512 devices in a mesh: tun: 128 (over z_lo, x, y, core), sec: 4 (over z_hi).
Axes of the slice: x: 4, y: 4, z: 16 (z_hi: 4, z_lo: 4; z = z_hi * 4 + z_lo), core: 2. Of those that a mesh axis runs over, the one named last changes fastest.
Arguments:
- wind_vector: float32 [3, 1024, 64, 128], P(None, 'tun', 'sec'), may hold values from -3 to 3
- thermal_surplus: float32 [1024, 64, 128], P('tun', 'sec'), may hold values from -4 to 4
- carbon_particulate: float32 [1024, 64, 128], P('tun', 'sec'), may hold values from 0 to 1
- particle_bin_weight: float32 [16, 1024, 64, 128], P(None, 'tun', 'sec'), may hold values from 0 to 1
- particle_bin_tally: int32 [1024, 64, 128], P('tun', 'sec'), may hold values from 0 to 16
- spray_region_label: int32 [1024, 64, 128], P('tun', 'sec'), may hold values from 0 to 8
- nozzle_onset_step: int32 [8], replicated, may hold values from 0 to 2
Outputs:
- velocity_out: float32 [3, 1024, 64, 128], P(None, 'tun', 'sec')
- temperature_out: float32 [1024, 64, 128], P('tun', 'sec')
- soot_out: float32 [1024, 64, 128], P('tun', 'sec')
- mass_out: float32 [16, 1024, 64, 128], P(None, 'tun', 'sec')
- count_out: int32 [1024, 64, 128], P('tun', 'sec')
The draws below stay inside these ranges and needn't reach their ends.
Inputs may be any that keep to these rules, and one draw needn't show every extreme that they name: A cell's live slots are its first particle_bin_tally slots.
All inputs are finite; a program needn't handle non-finite values.
Results may differ from the reference program's by a relative error of at most 0.0003.
Values sent between devices are 32-bit elements; how exact they have to be, the bound alone decides.
No kernel may reach another device: no remote copies, remote signals or barrier semaphores. Data moves between devices by JAX's collectives and lax.ppermute only.
A program may use at most 64 MiB of HBM per device.

```python
import jax
import jax.numpy as jnp
from jax import lax

VERTICAL_EXTENT = 128
DS = 16
NZONE = 8
TUNNELWISE_SIZE = 1024
LATERAL_EXTENT = 64


def set_ends(values, own_key, least, high):
    spot = [jax.random.randint(jax.random.fold_in(own_key, axis), (), 0, length) for axis, length in enumerate(values.shape)]
    main_axis = values.shape.index(max(values.shape))
    beside = spot[:main_axis] + [(spot[main_axis] + 1) % values.shape[main_axis]] + spot[main_axis + 1:]
    return values.at[tuple(spot)].set(least).at[tuple(beside)].set(high)


def level_of(stream_key, extent, shards, low, high):
    def one(position, parts):
        steps = jax.random.uniform(jax.random.fold_in(jax.random.fold_in(stream_key, 6), position), (parts,), jnp.float32, low / len(shards), high / len(shards))
        return jnp.repeat(jnp.exp(steps), extent[position] // parts).reshape((-1,) + (1,) * (len(extent) - position - 1))

    level = one(*shards[0])
    for cut in shards[1:]:
        level = level * one(*cut)
    return level


def gaussian(own_key, extent, deviation, reach, split=(), kind=jnp.bfloat16):
    values = deviation * jax.random.normal(own_key, extent, jnp.float32)
    if split:
        values = values * level_of(own_key, extent, split, -0.22, 0.18)
    return jnp.clip(values, -reach, reach).astype(kind)


def setup_inputs(seed: int = 0) -> dict:
    streams_of = jax.random.split(jax.random.key(seed), 8)
    wind_vector = gaussian(streams_of[0], (3, TUNNELWISE_SIZE, LATERAL_EXTENT, VERTICAL_EXTENT), 0.5, 3.0, ((1, 128), (2, 4)), jnp.float32)
    thermal_surplus = gaussian(streams_of[1], (TUNNELWISE_SIZE, LATERAL_EXTENT, VERTICAL_EXTENT), 1.0, 4.0, ((0, 128), (1, 4)), jnp.float32)
    carbon_particulate = jnp.clip(1.0 * jax.random.uniform(streams_of[2], (TUNNELWISE_SIZE, LATERAL_EXTENT, VERTICAL_EXTENT), jnp.float32) ** level_of(streams_of[2], (TUNNELWISE_SIZE, LATERAL_EXTENT, VERTICAL_EXTENT), ((0, 128), (1, 4)), -0.2, 0.2), 0.0, 1.0)
    particle_bin_weight = jnp.clip(1.0 * jax.random.uniform(streams_of[3], (DS, TUNNELWISE_SIZE, LATERAL_EXTENT, VERTICAL_EXTENT), jnp.float32) ** level_of(streams_of[3], (DS, TUNNELWISE_SIZE, LATERAL_EXTENT, VERTICAL_EXTENT), ((1, 128), (2, 4)), -0.2, 0.2), 0.0, 1.0)
    particle_bin_tally = set_ends(jax.random.randint(streams_of[4], (TUNNELWISE_SIZE, LATERAL_EXTENT, VERTICAL_EXTENT), 0, DS + 1), jax.random.fold_in(streams_of[4], 1), 0, DS).astype(jnp.int32)
    spray_region_label = set_ends(jax.random.randint(streams_of[5], (TUNNELWISE_SIZE, LATERAL_EXTENT, VERTICAL_EXTENT), 0, NZONE + 1), jax.random.fold_in(streams_of[5], 1), 0, NZONE).astype(jnp.int32)
    nozzle_onset_step = set_ends(jax.random.randint(streams_of[6], (NZONE,), 0, 3), jax.random.fold_in(streams_of[6], 1), 0, 2).astype(jnp.int32)
    return {"wind_vector": wind_vector, "thermal_surplus": thermal_surplus, "carbon_particulate": carbon_particulate, "particle_bin_weight": particle_bin_weight, "particle_bin_tally": particle_bin_tally, "spray_region_label": spray_region_label, "nozzle_onset_step": nozzle_onset_step}


visc_base = 0.2
time_step = 0.1
buoyancy = 0.5
drag_rate = 0.3
vent_speed = 1.0
inject_rate = 0.5
evap_rate = 0.4
latent_heat = 0.5
scavenge = 0.3


def neighbour(array, dim, offset):
    result = array
    lead = array.ndim - 3
    for split_axis in range(3):
        full = array.shape[lead + split_axis]
        start = 1 + offset if split_axis == dim else 1
        result = lax.slice_in_dim(result, start, start + full - 2, axis=lead + split_axis)
    return result


def advance(padded):
    centre = neighbour(padded, 0, 0)
    viscous = visc_base * (1.0 + 0.5 * jnp.tanh(padded[3]))
    visc_centre = neighbour(viscous, 0, 0)
    diffusion = jnp.zeros_like(centre)
    advection = jnp.zeros_like(centre)
    for dim in range(3):
        upper = neighbour(padded, dim, 1)
        lower = neighbour(padded, dim, -1)
        diffusion = diffusion + 0.5 * (visc_centre + neighbour(viscous, dim, 1)) * (upper - centre)
        diffusion = diffusion + 0.5 * (visc_centre + neighbour(viscous, dim, -1)) * (lower - centre)
        advection = advection + 0.5 * centre[dim] * (upper - lower)
    fresh = centre + time_step * (diffusion - advection)
    along = fresh[0] + time_step * drag_rate * (vent_speed - centre[0])
    upward = fresh[2] + time_step * buoyancy * centre[3]
    return jnp.stack([along, fresh[1], upward, fresh[3], fresh[4]])


def mist(transport_state, mass, count, spray_region_label, nozzle_onset_step, substep):
    slots = jnp.arange(mass.shape[0], dtype=jnp.int32)
    live = (slots[:, None, None, None] < count[None]).astype(jnp.float32)
    zones = jnp.arange(1, nozzle_onset_step.shape[0] + 1, dtype=jnp.int32)
    spraying = (nozzle_onset_step <= substep).astype(jnp.float32)
    zone_hit = (spray_region_label[None] == zones[:, None, None, None]).astype(jnp.float32)
    active = jnp.sum(zone_hit * spraying[:, None, None, None], axis=0)
    mass = mass + inject_rate * live * active[None]
    loaded = jnp.sum(live * mass, axis=0)
    evaporated = evap_rate * live * mass * jax.nn.sigmoid(transport_state[3])[None]
    heat = transport_state[3] - latent_heat * jnp.sum(evaporated, axis=0)
    sooty = transport_state[4] / (1.0 + scavenge * loaded)
    transport_state = jnp.stack([transport_state[0], transport_state[1], transport_state[2], heat, sooty])
    return transport_state, mass - evaporated


def reference(wind_vector, thermal_surplus, carbon_particulate, particle_bin_weight, particle_bin_tally, spray_region_label, nozzle_onset_step):
    transport_state = jnp.concatenate([wind_vector, thermal_surplus[None], carbon_particulate[None]], axis=0)
    mass, count = particle_bin_weight, particle_bin_tally
    for substep in range(2):
        padded = jnp.pad(transport_state, ((0, 0), (1, 1), (1, 1), (1, 1)))
        transport_state = advance(padded)
        mass = jnp.pad(mass, ((0, 0), (1, 0), (0, 0), (0, 0)))[:, :-1]
        count = jnp.pad(count, ((1, 0), (0, 0), (0, 0)))[:-1]
        transport_state, mass = mist(transport_state, mass, count, spray_region_label, nozzle_onset_step, substep)
    return transport_state[0:3], transport_state[3], transport_state[4], mass, count
```

```python
import jax
import jax.numpy as jnp
from jax import lax
from jax.experimental import pallas as pl
from jax.experimental.pallas import tpu as pltpu
from jax.sharding import PartitionSpec as P

visc_base = 0.2
time_step = 0.1
buoyancy = 0.5
drag_rate = 0.3
vent_speed = 1.0
inject_rate = 0.5
evap_rate = 0.4
latent_heat = 0.5
scavenge = 0.3

NF = 5
F32 = jnp.float32
VMEM = pl.BlockSpec(memory_space=pltpu.VMEM)
SMEM = pl.BlockSpec(memory_space=pltpu.SMEM)
ANY = pl.BlockSpec(memory_space=pl.ANY)
ROW = 8


def copies(pairs, sems):
    started = []
    for n, (src, dst) in enumerate(pairs):
        copy = pltpu.make_async_copy(src, dst, sems.at[n])
        copy.start()
        started.append(copy)
    return started


def live_sum(mass, count):
    total = jnp.zeros(count.shape, F32)
    for k in range(mass.shape[0]):
        total = total + jnp.where(count > k, mass[k], 0.0)
    return total


def pack_tun_kernel(wind, heat, soot, mass, count, label, msg_a, msg_b, total, fields, masses, counts, labels, sems):
    depth = heat.shape[0]
    pending = copies(
        [
            (mass, masses),
            (count, counts),
            (wind, fields.at[0:3]),
            (heat, fields.at[3]),
            (soot, fields.at[4]),
            (label, labels),
        ],
        sems,
    )
    odd = lax.axis_index("tun") % 2
    high = depth - 2
    start_a = jnp.where(odd == 1, 0, high)
    start_b = high - start_a
    for copy in pending[1:]:
        copy.wait()
    for start, msg in ((start_a, msg_a), (start_b, msg_b)):
        for f in range(NF):
            msg[f] = fields[f, pl.ds(start, 2)]
        msg[NF] = labels[pl.ds(start, 2)].astype(F32)
        msg[NF + 1] = counts[pl.ds(start, 2)].astype(F32)
    pending[0].wait()
    for x in range(depth):
        total[x] = live_sum(masses[:, x], counts[x])
    for start, msg in ((start_a, msg_a), (start_b, msg_b)):
        msg[NF + 2] = total[pl.ds(start, 2)]


def pack_tun(wind, heat, soot, mass, count, label):
    block = heat.shape
    msg = jax.ShapeDtypeStruct((NF + 3, 2) + block[1:], F32)
    return pl.pallas_call(
        pack_tun_kernel,
        out_shape=(msg, msg, jax.ShapeDtypeStruct(block, F32)),
        in_specs=[ANY] * 6,
        out_specs=(VMEM,) * 3,
        scratch_shapes=[
            pltpu.VMEM((NF,) + block, F32),
            pltpu.VMEM(mass.shape, F32),
            pltpu.VMEM(block, jnp.int32),
            pltpu.VMEM(block, jnp.int32),
            pltpu.SemaphoreType.DMA((6,)),
        ],
        name="pack_tun",
    )(wind, heat, soot, mass, count, label)


def onset_of(label, onset):
    first = jnp.full(label.shape, 1 << 20, jnp.int32)
    for z in range(onset.shape[0]):
        first = jnp.where(label == z + 1, onset[z], first)
    return first


def pack_sec_kernel(onset, wind, heat, soot, count, label, total, got_a, got_b, to_low, to_high, up, down):
    depth, rows = heat.shape[0], heat.shape[1]
    odd = lax.axis_index("tun") % 2 == 1
    for n in range(NF + 3):
        up[n] = jnp.where(odd, got_a[n], got_b[n])
        down[n] = jnp.where(odd, got_b[n], got_a[n])
    fields = [wind.at[0], wind.at[1], wind.at[2], heat, soot]
    for msg, first, second in ((to_low, 0, 1), (to_high, rows - 1, rows - 2)):
        for f in range(NF):
            for n, row in ((f, first), (NF + f, second)):
                msg[n, 0:2, :] = up[f, :, row, :]
                msg[n, 2 : 2 + depth, :] = fields[f][:, row, :]
                msg[n, 2 + depth : 4 + depth, :] = down[f, :, row, :]
        counts = count[:, first, :].astype(F32)
        sums = total[:, first, :]
        counts = jnp.concatenate([up[NF + 1, 1, first : first + 1, :], counts[: depth - 1]], axis=0)
        sums = jnp.concatenate([up[NF + 2, 1, first : first + 1, :], sums[: depth - 1]], axis=0)
        sprays = onset_of(label[:, first, :], onset) <= 0
        msg[2 * NF, 2 : 2 + depth, :] = sums + jnp.where(sprays, inject_rate * counts, 0.0)


def pack_sec(onset, wind, heat, soot, count, label, total, got_a, got_b):
    depth, rows, lanes = heat.shape
    msg = jax.ShapeDtypeStruct((2 * NF + 1, depth + 4, lanes), F32)
    halo = jax.ShapeDtypeStruct(got_a.shape, F32)
    return pl.pallas_call(
        pack_sec_kernel,
        out_shape=(msg, msg, halo, halo),
        in_specs=[SMEM] + [VMEM] * 8,
        out_specs=(VMEM,) * 4,
        name="pack_sec",
    )(onset, wind, heat, soot, count, label, total, got_a, got_b)


def pack_mass_kernel(mass, after, msg, sem):
    depth = mass.shape[1]
    copy = pltpu.make_async_copy(mass.at[:, depth - 2 : depth], msg, sem)
    copy.start()
    copy.wait()


def pack_mass(mass, after):
    return pl.pallas_call(
        pack_mass_kernel,
        out_shape=jax.ShapeDtypeStruct((mass.shape[0], 2) + mass.shape[2:], F32),
        in_specs=[ANY, ANY],
        out_specs=VMEM,
        scratch_shapes=[pltpu.SemaphoreType.DMA(())],
        name="pack_mass",
    )(mass, after)


def viscosity(heat):
    return visc_base * (1.0 + 0.5 * jnp.tanh(heat))


def stencil(centre, nu, sides, nu_sides):
    lane = lax.broadcasted_iota(jnp.int32, nu.shape, 1)
    last = nu.shape[1] - 1
    rest = None
    weights = []
    for d in range(3):
        for side, sign in ((0, -1.0), (1, 1.0)):
            weight = (0.5 * time_step) * ((nu + nu_sides[d][side]) - sign * centre[d])
            rest = weight if rest is None else rest + weight
            if d == 2:
                weight = jnp.where(lane == (last if side else 0), 0.0, weight)
            weights.append(weight)
    rest = 1.0 - rest
    out = []
    for f in range(NF):
        value = rest * centre[f]
        for d in range(3):
            for side in (0, 1):
                value = value + weights[2 * d + side] * sides[d][side](f)
        out.append(value)
    out[0] = out[0] + (time_step * drag_rate) * (vent_speed - centre[0])
    out[2] = out[2] + (time_step * buoyancy) * centre[3]
    return out


def around(plane):
    return pltpu.roll(plane, 1, 1), pltpu.roll(plane, plane.shape[1] - 1, 1)


def nu_around(nu):
    lane = lax.broadcasted_iota(jnp.int32, nu.shape, 1)
    low, high = around(nu)
    return jnp.where(lane == 0, visc_base, low), jnp.where(lane == nu.shape[1] - 1, visc_base, high)


def tail_kernel(
    onset, wind, heat, soot, mass, count, label, total, up, down, to_low, to_high, low, high, above,
    wind_out, heat_out, soot_out, mass_out, count_out,
    ext, ext_nu, nxt, nxt_nu, damp, loads, fields, masses, counts, sems,
):
    depth, rows, lanes = heat.shape
    slots = mass.shape[0]
    tun, sec = lax.axis_index("tun"), lax.axis_index("sec")
    inside_up, inside_down = tun > 0, tun < lax.axis_size("tun") - 1
    inside_low, inside_high = sec > 0, sec < lax.axis_size("sec") - 1
    body = slice(ROW, ROW + rows)
    own = [wind.at[0], wind.at[1], wind.at[2], heat, soot]

    for f in range(NF):
        for x in range(depth + 4):
            if x < 2:
                plane = up[f, x]
            elif x < depth + 2:
                plane = own[f][x - 2]
            else:
                plane = down[f, x - depth - 2]
            ext[f, x, body, :] = plane
            if f == 3:
                ext_nu[x, body, :] = viscosity(plane)
        for x in range(1, depth + 3):
            ext[f, x, ROW - 1 : ROW, :] = low[f, x : x + 1, :]
            ext[f, x, ROW + rows : ROW + rows + 1, :] = high[f, x : x + 1, :]
    nu_low, nu_high = viscosity(low[3]), viscosity(high[3])
    for x in range(1, depth + 3):
        ext_nu[x, ROW - 1 : ROW, :] = nu_low[x : x + 1, :]
        ext_nu[x, ROW + rows : ROW + rows + 1, :] = nu_high[x : x + 1, :]

    def first(x):
        return onset_of(label[x], onset)

    for x in range(-1, depth + 1):
        centre = [ext[f, x + 2, body, :] for f in range(NF)]
        nu = ext_nu[x + 2, body, :]
        lifted = [around(c) for c in centre]
        sides = [
            (lambda f: ext[f, x + 1, body, :], lambda f: ext[f, x + 3, body, :]),
            (lambda f: ext[f, x + 2, ROW - 1 : ROW + rows - 1, :], lambda f: ext[f, x + 2, ROW + 1 : ROW + rows + 1, :]),
            (lambda f: lifted[f][0], lambda f: lifted[f][1]),
        ]
        nu_sides = [
            (ext_nu[x + 1, body, :], ext_nu[x + 3, body, :]),
            (ext_nu[x + 2, ROW - 1 : ROW + rows - 1, :], ext_nu[x + 2, ROW + 1 : ROW + rows + 1, :]),
            nu_around(nu),
        ]
        new = stencil(centre, nu, sides, nu_sides)
        if x < 1:
            moved_total, moved_count = up[NF + 2, x + 1], up[NF + 1, x + 1]
        else:
            moved_total, moved_count = total[x - 1], count[x - 1].astype(F32)
        if x < 0:
            zone = up[NF, 1].astype(jnp.int32)
        elif x < depth:
            zone = label[x]
        else:
            zone = down[NF, 0].astype(jnp.int32)
        sprays = jnp.where(onset_of(zone, onset) <= 0, inject_rate, 0.0)
        load = moved_total + sprays * moved_count
        evap = evap_rate * jax.nn.sigmoid(new[3])
        new[3] = new[3] - latent_heat * (evap * load)
        new[4] = new[4] / (1.0 + scavenge * load)
        if x < depth:
            damp[0, x + 1] = 1.0 - evap
            damp[1, x + 1] = sprays * (1.0 - evap)
            loads[x + 1] = load * (1.0 - evap)
        keep = inside_up if x < 0 else inside_down if x == depth else None
        for f in range(NF):
            value = new[f] if keep is None else jnp.where(keep, new[f], 0.0)
            nxt[f, x + 1, body, :] = value
            if f == 3:
                nxt_nu[x + 1, body, :] = viscosity(value)

    for got, sent, row, flip, keep in ((low, to_low, ROW - 1, False, inside_low), (high, to_high, ROW + rows, True, inside_high)):
        here = slice(2, 2 + depth)
        centre = [got[f, here, :] for f in range(NF)]
        nu_all = nu_high if flip else nu_low
        nu = nu_all[2 : 2 + depth]
        lifted = [around(c) for c in centre]
        inner = lambda f, sent=sent: sent[f, here, :]
        outer = lambda f, got=got: got[NF + f, here, :]
        nu_inner, nu_outer = viscosity(sent[3, here, :]), viscosity(got[NF + 3, here, :])
        sides = [
            (lambda f, got=got: got[f, 1 : 1 + depth, :], lambda f, got=got: got[f, 3 : 3 + depth, :]),
            (inner, outer) if flip else (outer, inner),
            (lambda f: lifted[f][0], lambda f: lifted[f][1]),
        ]
        nu_sides = [
            (viscosity(got[3, 1 : 1 + depth, :]), viscosity(got[3, 3 : 3 + depth, :])),
            (nu_inner, nu_outer) if flip else (nu_outer, nu_inner),
            nu_around(nu),
        ]
        new = stencil(centre, nu, sides, nu_sides)
        load = got[2 * NF, here, :]
        evap = evap_rate * jax.nn.sigmoid(new[3])
        new[3] = new[3] - latent_heat * (evap * load)
        new[4] = new[4] / (1.0 + scavenge * load)
        for f in range(NF):
            value = jnp.where(keep, new[f], 0.0)
            for x in range(depth):
                nxt[f, x + 1, row : row + 1, :] = value[x : x + 1]
            if f == 3:
                value = viscosity(value)
                for x in range(depth):
                    nxt_nu[x + 1, row : row + 1, :] = value[x : x + 1]

    pending = []
    for x in range(depth):
        centre = [nxt[f, x + 1, body, :] for f in range(NF)]
        nu = nxt_nu[x + 1, body, :]
        lifted = [around(c) for c in centre]
        sides = [
            (lambda f: nxt[f, x, body, :], lambda f: nxt[f, x + 2, body, :]),
            (lambda f: nxt[f, x + 1, ROW - 1 : ROW + rows - 1, :], lambda f: nxt[f, x + 1, ROW + 1 : ROW + rows + 1, :]),
            (lambda f: lifted[f][0], lambda f: lifted[f][1]),
        ]
        nu_sides = [
            (nxt_nu[x, body, :], nxt_nu[x + 2, body, :]),
            (nxt_nu[x + 1, ROW - 1 : ROW + rows - 1, :], nxt_nu[x + 1, ROW + 1 : ROW + rows + 1, :]),
            nu_around(nu),
        ]
        new = stencil(centre, nu, sides, nu_sides)
        moved = up[NF + 1, x].astype(jnp.int32) if x < 2 else count[x - 2]
        sprays = jnp.where(first(x) <= 1, inject_rate, 0.0)
        load = loads[x] + sprays * moved.astype(F32)
        evap = evap_rate * jax.nn.sigmoid(new[3])
        new[3] = new[3] - latent_heat * (evap * load)
        new[4] = new[4] / (1.0 + scavenge * load)
        for f in range(NF):
            fields[f, x] = new[f]
        counts[x] = moved
        scale = damp[0, x] * (1.0 - evap)
        gain = (damp[1, x] + sprays) * (1.0 - evap)
        for k in range(slots):
            before = above[k, x] if x < 2 else mass[k, x - 2]
            masses[k, x] = jnp.where(moved > k, before * scale + gain, before)
    pending = copies(
        [
            (masses, mass_out),
            (fields.at[0:3], wind_out),
            (fields.at[3], heat_out),
            (fields.at[4], soot_out),
            (counts, count_out),
        ],
        sems,
    )
    for copy in pending:
        copy.wait()


def tail(onset, wind, heat, soot, mass, count, label, total, up, down, to_low, to_high, low, high, above):
    depth, rows, lanes = heat.shape
    tall = rows + 2 * ROW
    return pl.pallas_call(
        tail_kernel,
        out_shape=(
            jax.ShapeDtypeStruct(wind.shape, F32),
            jax.ShapeDtypeStruct(heat.shape, F32),
            jax.ShapeDtypeStruct(heat.shape, F32),
            jax.ShapeDtypeStruct(mass.shape, F32),
            jax.ShapeDtypeStruct(heat.shape, jnp.int32),
        ),
        in_specs=[SMEM] + [VMEM] * 14,
        out_specs=(ANY,) * 5,
        scratch_shapes=[
            pltpu.VMEM((NF, depth + 4, tall, lanes), F32),
            pltpu.VMEM((depth + 4, tall, lanes), F32),
            pltpu.VMEM((NF, depth + 2, tall, lanes), F32),
            pltpu.VMEM((depth + 2, tall, lanes), F32),
            pltpu.VMEM((2, depth + 1, rows, lanes), F32),
            pltpu.VMEM((depth + 1, rows, lanes), F32),
            pltpu.VMEM((NF, depth, rows, lanes), F32),
            pltpu.VMEM(mass.shape, F32),
            pltpu.VMEM((depth, rows, lanes), jnp.int32),
            pltpu.SemaphoreType.DMA((5,)),
        ],
        name="tail",
    )(onset, wind, heat, soot, mass, count, label, total, up, down, to_low, to_high, low, high, above)


def local(wind, heat, soot, mass, count, label, onset):
    chain, width = lax.axis_size("tun"), lax.axis_size("sec")
    pairs_a = [(i, i ^ 1) for i in range(chain)]
    pairs_b = [(i, ((i + 1) ^ 1) - 1) for i in range(1, chain - 1)]
    msg_a, msg_b, total = pack_tun(wind, heat, soot, mass, count, label)
    got_a = lax.ppermute(msg_a, "tun", pairs_a)
    got_b = lax.ppermute(msg_b, "tun", pairs_b)
    to_low, to_high, up, down = pack_sec(onset, wind, heat, soot, count, label, total, got_a, got_b)
    low = lax.ppermute(to_high, "sec", [(i, i + 1) for i in range(width - 1)])
    high = lax.ppermute(to_low, "sec", [(i + 1, i) for i in range(width - 1)])
    above = lax.ppermute(pack_mass(mass, up), "tun", [(i, i + 1) for i in range(chain - 1)])
    return tail(onset, wind, heat, soot, mass, count, label, total, up, down, to_low, to_high, low, high, above)


def solution(mesh):
    return jax.shard_map(
        local,
        mesh=mesh,
        in_specs=(
            P(None, "tun", "sec", None),
            P("tun", "sec", None),
            P("tun", "sec", None),
            P(None, "tun", "sec", None),
            P("tun", "sec", None),
            P("tun", "sec", None),
            P(),
        ),
        out_specs=(
            P(None, "tun", "sec", None),
            P("tun", "sec", None),
            P("tun", "sec", None),
            P(None, "tun", "sec", None),
            P("tun", "sec", None),
        ),
        check_vma=False,
    )
```

```python
import jax
import jax.numpy as jnp
from jax import lax
from jax.experimental import pallas as pl
from jax.experimental.pallas import tpu as pltpu
from jax.sharding import PartitionSpec as P

visc_base = 0.2
time_step = 0.1
buoyancy = 0.5
drag_rate = 0.3
vent_speed = 1.0
inject_rate = 0.5
evap_rate = 0.4
latent_heat = 0.5
scavenge = 0.3

NF = 5
F32 = jnp.float32
VMEM = pl.BlockSpec(memory_space=pltpu.VMEM)
SMEM = pl.BlockSpec(memory_space=pltpu.SMEM)
HBM = pl.BlockSpec(memory_space=pltpu.HBM)
ANY = pl.BlockSpec(memory_space=pl.ANY)
ROW = 8


FIRST_COST, LAST_COST = 0, 100


def cost(units):
    return pl.CostEstimate(flops=int(units * 1e9), transcendentals=0, bytes_accessed=int(units * 1e6))


LIMIT = pltpu.CompilerParams(vmem_limit_bytes=12 << 20)


def on_chip(*arrays):
    return tuple(pltpu.with_memory_space_constraint(a, pltpu.VMEM) for a in arrays)


def copies(pairs, sems):
    started = []
    for n, (src, dst) in enumerate(pairs):
        copy = pltpu.make_async_copy(src, dst, sems.at[n])
        copy.start()
        started.append(copy)
    return started

def live_sum(mass, count):
    total = jnp.zeros(count.shape, F32)
    for k in range(len(mass)):
        total = total + jnp.where(count > k, mass[k], 0.0)
    return total


def onset_of(label, onset):
    first = jnp.full(label.shape, 1 << 20, jnp.int32)
    for z in range(onset.shape[0]):
        first = jnp.where(label == z + 1, onset[z], first)
    return first


def pack_tun_kernel(
    onset, wind, heat, soot, mass, count, label, msg_b, msg_a, masses, counts, labels, onsets, sems
):
    depth = heat.shape[0]
    odd = lax.axis_index("tun") % 2 == 1
    top = depth - 2
    start_a = jnp.where(odd, 0, top)
    start_b = top - start_a
    pairs = [(onset, onsets), (mass.at[:, top:depth], masses), (count.at[top:depth], counts)]
    for n, (start, msg) in enumerate(((start_b, msg_b), (start_a, msg_a))):
        here = pl.ds(start, 2)
        pairs += [
            (label.at[here], labels.at[n]),
            (wind.at[:, here], msg.at[0:3]),
            (heat.at[here], msg.at[3]),
            (soot.at[here], msg.at[4]),
        ]
    for copy in copies(pairs, sems):
        copy.wait()
    held = counts[...]
    total = live_sum([masses[k] for k in range(masses.shape[0])], held)
    for n, msg in enumerate((msg_b, msg_a)):
        msg[NF] = onset_of(labels[n], onsets).astype(F32)
        msg[NF + 1] = held.astype(F32)
        msg[NF + 2] = total


def in_hbm(*arrays):
    return tuple(pltpu.with_memory_space_constraint(a, pltpu.HBM) for a in arrays)


def pack_tun(onset, wind, heat, soot, mass, count, label):
    plane = heat.shape[1:]
    msg = pltpu.VMEM((NF + 3, 2) + plane, F32)
    return pl.pallas_call(
        pack_tun_kernel,
        out_shape=(msg, msg),
        in_specs=[HBM] * 7,
        out_specs=(VMEM,) * 2,
        scratch_shapes=[
            pltpu.VMEM((mass.shape[0], 2) + plane, F32),
            pltpu.VMEM((2,) + plane, jnp.int32),
            pltpu.VMEM((2, 2) + plane, jnp.int32),
            pltpu.SMEM(onset.shape, jnp.int32),
            pltpu.SemaphoreType.DMA((11,)),
        ],
        compiler_params=LIMIT,
        name="pack_tun",
    )(*in_hbm(onset, wind, heat, soot, mass, count, label))


def load_kernel(onset, wind, heat, soot, mass, count, label, after, winds, heats, soots, masses, counts, begins, labels, onsets, sems):
    pairs = [
        (onset, onsets), (label, labels), (mass, masses), (wind, winds), (heat, heats), (soot, soots), (count, counts)
    ]
    pending = copies(pairs, sems)
    pending[0].wait()
    pending[1].wait()
    for x in range(label.shape[0]):
        begins[x] = onset_of(labels[x], onsets)
    for copy in pending[2:]:
        copy.wait()


def load(onset, wind, heat, soot, mass, count, label, after):
    arrays = (wind, heat, soot, mass, count, label)
    return pl.pallas_call(
        load_kernel,
        out_shape=tuple(pltpu.VMEM(a.shape, a.dtype) for a in arrays),
        in_specs=[HBM] * 7 + [ANY],
        out_specs=(VMEM,) * 6,
        scratch_shapes=[
            pltpu.VMEM(label.shape, jnp.int32),
            pltpu.SMEM(onset.shape, jnp.int32),
            pltpu.SemaphoreType.DMA((7,)),
        ],
        compiler_params=LIMIT,
        name="load",
    )(*in_hbm(onset, *arrays), after)


def pack_mass_kernel(mass, after, msg):
    depth = mass.shape[1]
    for k in range(mass.shape[0]):
        msg[k] = mass[k, depth - 2 : depth]


def pack_mass(mass, after):
    return pl.pallas_call(
        pack_mass_kernel,
        out_shape=pltpu.VMEM((mass.shape[0], 2) + mass.shape[2:], F32),
        in_specs=[VMEM] * 2,
        out_specs=VMEM,
        compiler_params=LIMIT,
        name="pack_mass",
    )(*on_chip(mass, after))


def pack_sec_kernel(got_b, got_a, wind, heat, soot, mass, count, begins, to_low, to_high):
    depth, rows, lanes = heat.shape
    slots = mass.shape[0]
    odd = lax.axis_index("tun") % 2 == 1

    def flat(ref):
        return ref.reshape(-1, lanes)

    winds, heats, soots, massed = flat(wind), flat(heat), flat(soot), flat(mass)
    counted, begun, from_a, from_b = flat(count), flat(begins), flat(got_a), flat(got_b)

    def own(f, row):
        ref, base = ((winds, f * depth * rows), (heats, 0), (soots, 0))[max(f - 2, 0)]
        return ref[pl.ds(base + row, depth, stride=rows), :]

    def beside(f, row):
        here = pl.ds(f * 2 * rows + row, 2, stride=rows)
        a, b = from_a[here, :], from_b[here, :]
        return jnp.where(odd, a, b), jnp.where(odd, b, a)

    for msg, first, second in ((to_low, 0, 1), (to_high, rows - 1, rows - 2)):
        for f in range(NF):
            for n, row in ((f, first), (NF + f, second)):
                before, after = beside(f, row)
                msg[n] = jnp.concatenate([before, own(f, row), after], axis=0)
        here = pl.ds(first, depth, stride=rows)
        held = counted[here, :]
        sums = live_sum([massed[pl.ds(k * depth * rows + first, depth, stride=rows), :] for k in range(slots)], held)
        begins_up, begins_down = beside(NF, first)
        held_up, _ = beside(NF + 1, first)
        sums_up, _ = beside(NF + 2, first)
        starts = jnp.concatenate([begins_up[1:], begun[here, :].astype(F32), begins_down[:1]], axis=0)
        held = jnp.concatenate([held_up, held.astype(F32)], axis=0)
        sums = jnp.concatenate([sums_up, sums], axis=0)
        msg[2 * NF, 1 : 3 + depth, :] = sums + jnp.where(starts <= 0.0, inject_rate * held, 0.0)


def pack_sec(wind, heat, soot, mass, count, begins, got_a, got_b):
    depth, rows, lanes = heat.shape
    msg = pltpu.VMEM((2 * NF + 1, depth + 4, lanes), F32)
    return pl.pallas_call(
        pack_sec_kernel,
        out_shape=(msg, msg),
        in_specs=[VMEM] * 8,
        out_specs=(VMEM,) * 2,
        compiler_params=LIMIT,
        name="pack_sec",
    )(*on_chip(got_b, got_a, wind, heat, soot, mass, count, begins))


def viscosity(heat):
    return visc_base * (1.0 + 0.5 * jnp.tanh(heat))


def stencil(centre, nu, sides, nu_sides):
    lane = lax.broadcasted_iota(jnp.int32, nu.shape, 1)
    last = nu.shape[1] - 1
    rest = None
    weights = []
    for d in range(3):
        for side, sign in ((0, -1.0), (1, 1.0)):
            weight = (0.5 * time_step) * ((nu + nu_sides[d][side]) - sign * centre[d])
            rest = weight if rest is None else rest + weight
            if d == 2:
                weight = jnp.where(lane == (last if side else 0), 0.0, weight)
            weights.append(weight)
    rest = 1.0 - rest
    out = []
    for f in range(NF):
        value = rest * centre[f]
        for d in range(3):
            for side in (0, 1):
                value = value + weights[2 * d + side] * sides[d][side](f)
        out.append(value)
    out[0] = out[0] + (time_step * drag_rate) * (vent_speed - centre[0])
    out[2] = out[2] + (time_step * buoyancy) * centre[3]
    return out


def around(plane):
    return pltpu.roll(plane, 1, 1), pltpu.roll(plane, plane.shape[1] - 1, 1)


def nu_around(nu):
    lane = lax.broadcasted_iota(jnp.int32, nu.shape, 1)
    low, high = around(nu)
    return jnp.where(lane == 0, visc_base, low), jnp.where(lane == nu.shape[1] - 1, visc_base, high)


def first_kernel(
    wind, heat, soot, mass, count, begins, got_a, got_b, after,
    count_out, nxt, nxt_nu, keep, loads, spray_0, spray_1,
    ext, ext_nu, counts, sems,
):
    depth, rows, lanes = heat.shape
    slots = mass.shape[0]
    tall = rows + 2 * ROW
    tun = lax.axis_index("tun")
    odd = tun % 2 == 1
    own = [wind.at[0], wind.at[1], wind.at[2], heat, soot]

    def beside(n, x):
        return jnp.where(odd, got_a[n, x], got_b[n, x]), jnp.where(odd, got_b[n, x], got_a[n, x])

    def put(ref, plane, value):
        ref[plane * tall + ROW : plane * tall + ROW + rows, :] = value

    def at(ref, plane, shift=0):
        return ref[plane * tall + ROW + shift : plane * tall + ROW + shift + rows, :]

    planes = depth + 4
    for f in range(NF):
        for x in range(depth):
            put(ext, f * planes + x + 2, own[f][x])
        for x in (0, 1):
            before, behind = beside(f, x)
            put(ext, f * planes + x, before)
            put(ext, f * planes + depth + 2 + x, behind)
    for x in range(planes):
        put(ext_nu, x, viscosity(at(ext, 3 * planes + x)))

    for x in (0, 1):
        counts[x] = beside(NF + 1, x)[0].astype(jnp.int32)
    for x in range(depth - 2):
        counts[x + 2] = count[x]
    pending = copies([(counts, count_out)], sems)

    for x in range(-1, depth + 1):
        centre = [at(ext, f * planes + x + 2) for f in range(NF)]
        nu = at(ext_nu, x + 2)
        lifted = [around(c) for c in centre]
        sides = [
            (lambda f: at(ext, f * planes + x + 1), lambda f: at(ext, f * planes + x + 3)),
            (lambda f: at(ext, f * planes + x + 2, -1), lambda f: at(ext, f * planes + x + 2, 1)),
            (lambda f: lifted[f][0], lambda f: lifted[f][1]),
        ]
        nu_sides = [
            (at(ext_nu, x + 1), at(ext_nu, x + 3)),
            (at(ext_nu, x + 2, -1), at(ext_nu, x + 2, 1)),
            nu_around(nu),
        ]
        new = stencil(centre, nu, sides, nu_sides)
        if x < 1:
            moved_total, moved_count = beside(NF + 2, x + 1)[0], beside(NF + 1, x + 1)[0]
        else:
            held = count[x - 1]
            moved_total, moved_count = live_sum([mass[k, x - 1] for k in range(slots)], held), held.astype(F32)
        if x < 0:
            start = beside(NF, 1)[0].astype(jnp.int32)
        elif x < depth:
            start = begins[x]
        else:
            start = beside(NF, 0)[1].astype(jnp.int32)
        sprays = jnp.where(start <= 0, inject_rate, 0.0)
        load = moved_total + sprays * moved_count
        evap = evap_rate * jax.nn.sigmoid(new[3])
        new[3] = new[3] - latent_heat * (evap * load)
        new[4] = new[4] / (1.0 + scavenge * load)
        if x < depth:
            keep[(x + 1) * rows : (x + 2) * rows, :] = 1.0 - evap
            loads[x + 1] = load
            spray_0[x + 1] = sprays
        if 0 <= x < depth:
            spray_1[x] = jnp.where(start <= 1, inject_rate, 0.0)
        inside = tun > 0 if x < 0 else tun < lax.axis_size("tun") - 1 if x == depth else None
        for f in range(NF):
            value = new[f] if inside is None else jnp.where(inside, new[f], 0.0)
            put(nxt, f * (depth + 2) + x + 1, value)
            if f == 3:
                put(nxt_nu, x + 1, viscosity(value))
    for copy in pending:
        copy.wait()


def first(wind, heat, soot, mass, count, begins, got_a, got_b, after):
    depth, rows, lanes = heat.shape
    tall = rows + 2 * ROW
    return pl.pallas_call(
        first_kernel,
        out_shape=(
            jax.ShapeDtypeStruct(count.shape, jnp.int32),
            pltpu.VMEM((NF * (depth + 2) * tall, lanes), F32),
            pltpu.VMEM(((depth + 2) * tall, lanes), F32),
            pltpu.VMEM(((depth + 1) * rows, lanes), F32),
            pltpu.VMEM((depth + 1, rows, lanes), F32),
            pltpu.VMEM((depth + 1, rows, lanes), F32),
            pltpu.VMEM((depth, rows, lanes), F32),
        ),
        in_specs=[VMEM] * 8 + [ANY],
        out_specs=(ANY,) + (VMEM,) * 6,
        scratch_shapes=[
            pltpu.VMEM((NF * (depth + 4) * tall, lanes), F32),
            pltpu.VMEM(((depth + 4) * tall, lanes), F32),
            pltpu.VMEM((depth, rows, lanes), jnp.int32),
            pltpu.SemaphoreType.DMA((1,)),
        ],
        compiler_params=LIMIT,
        cost_estimate=cost(FIRST_COST),
        name="first_substep",
    )(*on_chip(wind, heat, soot, mass, count, begins, got_a, got_b), after)


def last_kernel(
    high, low, to_low, to_high, count, got_a, got_b, loads, spray_0, spray_1, nxt_in, nxt_nu_in, keep_in,
    wind_out, heat_out, soot_out, scale, gain, moved, nxt, nxt_nu, keep,
    fields, sems,
):
    depth, rows, lanes = count.shape
    tall = rows + 2 * ROW
    planes = depth + 2
    tun, sec = lax.axis_index("tun"), lax.axis_index("sec")
    odd = tun % 2 == 1
    inside_up, inside_down = tun > 0, tun < lax.axis_size("tun") - 1
    sides_of = (
        (low, to_low, ROW - 1, 0, sec > 0),
        (high, to_high, ROW + rows, rows - 1, sec < lax.axis_size("sec") - 1),
    )

    place = lax.broadcasted_iota(jnp.int32, (planes, lanes), 0)
    inside = ((place > 0) | inside_up) & ((place < planes - 1) | inside_down)
    mid = slice(1, 1 + planes)
    for flip, (got, sent, outer_row, inner_row, there) in enumerate(sides_of):
        got_nu, sent_nu = viscosity(got[3]), viscosity(sent[3])
        got_nu_2, sent_nu_2 = viscosity(got[NF + 3, mid, :]), viscosity(sent[NF + 3, mid, :])
        for ref, ref_nu, near, near_nu, far, far_nu, row, valid in (
            (got, got_nu, lambda f, sent=sent: sent[f, mid, :], sent_nu[mid], lambda f, got=got: got[NF + f, mid, :], got_nu_2, outer_row, there),
            (sent, sent_nu, lambda f, got=got: got[f, mid, :], got_nu[mid], lambda f, sent=sent: sent[NF + f, mid, :], sent_nu_2, ROW + inner_row, inside),
        ):
            is_outer = ref is got
            centre = [ref[f, mid, :] for f in range(NF)]
            nu = ref_nu[mid]
            lifted = [around(c) for c in centre]
            swap = bool(flip) == is_outer
            sides = [
                (lambda f, ref=ref: ref[f, 0:planes, :], lambda f, ref=ref: ref[f, 2 : 2 + planes, :]),
                (near, far) if swap else (far, near),
                (lambda f: lifted[f][0], lambda f: lifted[f][1]),
            ]
            nu_sides = [
                (ref_nu[0:planes], ref_nu[2 : 2 + planes]),
                (near_nu, far_nu) if swap else (far_nu, near_nu),
                nu_around(nu),
            ]
            new = stencil(centre, nu, sides, nu_sides)
            load = ref[2 * NF, mid, :]
            evap = evap_rate * jax.nn.sigmoid(new[3])
            new[3] = new[3] - latent_heat * (evap * load)
            new[4] = new[4] / (1.0 + scavenge * load)
            for f in range(NF):
                value = jnp.where(valid, new[f], 0.0)
                nxt[pl.ds(f * planes * tall + row, planes, stride=tall), :] = value
                if f == 3:
                    nxt_nu[pl.ds(row, planes, stride=tall), :] = viscosity(value)
            if not is_outer:
                keep[pl.ds(inner_row, depth + 1, stride=rows), :] = (1.0 - evap)[: depth + 1]

    def at(ref, plane, shift=0):
        return ref[plane * tall + ROW + shift : plane * tall + ROW + shift + rows, :]

    for x in range(depth):
        centre = [at(nxt, f * planes + x + 1) for f in range(NF)]
        nu = at(nxt_nu, x + 1)
        lifted = [around(c) for c in centre]
        sides = [
            (lambda f: at(nxt, f * planes + x), lambda f: at(nxt, f * planes + x + 2)),
            (lambda f: at(nxt, f * planes + x + 1, -1), lambda f: at(nxt, f * planes + x + 1, 1)),
            (lambda f: lifted[f][0], lambda f: lifted[f][1]),
        ]
        nu_sides = [
            (at(nxt_nu, x), at(nxt_nu, x + 2)),
            (at(nxt_nu, x + 1, -1), at(nxt_nu, x + 1, 1)),
            nu_around(nu),
        ]
        new = stencil(centre, nu, sides, nu_sides)
        if x < 2:
            held = jnp.where(odd, got_a[NF + 1, x], got_b[NF + 1, x]).astype(jnp.int32)
        else:
            held = count[x - 2]
        kept = keep[x * rows : (x + 1) * rows, :]
        sprays = spray_1[x]
        load = loads[x] * kept + sprays * held.astype(F32)
        evap = evap_rate * jax.nn.sigmoid(new[3])
        new[3] = new[3] - latent_heat * (evap * load)
        new[4] = new[4] / (1.0 + scavenge * load)
        for f in range(NF):
            fields[f, x] = new[f]
        moved[x] = held
        scale[x] = kept * (1.0 - evap)
        gain[x] = (spray_0[x] * kept + sprays) * (1.0 - evap)
    for copy in copies([(fields.at[0:3], wind_out), (fields.at[3], heat_out), (fields.at[4], soot_out)], sems):
        copy.wait()


def last(high, low, to_low, to_high, count, got_a, got_b, loads, spray_0, spray_1, nxt, nxt_nu, keep):
    block = count.shape
    operands = on_chip(high, low, to_low, to_high, count, got_a, got_b, loads, spray_0, spray_1, nxt, nxt_nu, keep)
    return pl.pallas_call(
        last_kernel,
        out_shape=(
            jax.ShapeDtypeStruct((3,) + block, F32),
            jax.ShapeDtypeStruct(block, F32),
            jax.ShapeDtypeStruct(block, F32),
            pltpu.VMEM(block, F32),
            pltpu.VMEM(block, F32),
            pltpu.VMEM(block, jnp.int32),
            pltpu.VMEM(nxt.shape, F32),
            pltpu.VMEM(nxt_nu.shape, F32),
            pltpu.VMEM(keep.shape, F32),
        ),
        in_specs=[VMEM] * 13,
        out_specs=(ANY,) * 3 + (VMEM,) * 6,
        input_output_aliases={10: 6, 11: 7, 12: 8},
        scratch_shapes=[pltpu.VMEM((NF,) + block, F32), pltpu.SemaphoreType.DMA((3,))],
        compiler_params=LIMIT,
        cost_estimate=cost(LAST_COST),
        name="last_substep",
    )(*operands)[:6]


def droplets_kernel(mass, above, scale, gain, moved, mass_out, masses, sems):
    slots, depth = mass.shape[:2]
    pending = []
    for x in range(depth):
        held, by, plus = moved[x], scale[x], gain[x]
        for k in range(slots):
            before = above[k, x] if x < 2 else mass[k, x - 2]
            masses[k, x] = jnp.where(held > k, before * by + plus, before)
        copy = pltpu.make_async_copy(masses.at[:, x], mass_out.at[:, x], sems.at[x])
        copy.start()
        pending.append(copy)
    for copy in pending:
        copy.wait()


def droplets(mass, above, scale, gain, moved):
    return pl.pallas_call(
        droplets_kernel,
        out_shape=jax.ShapeDtypeStruct(mass.shape, F32),
        in_specs=[VMEM] * 5,
        out_specs=ANY,
        scratch_shapes=[pltpu.VMEM(mass.shape, F32), pltpu.SemaphoreType.DMA((mass.shape[1],))],
        compiler_params=LIMIT,
        name="droplets",
    )(*on_chip(mass, above, scale, gain, moved))


def local(wind, heat, soot, mass, count, label, onset):
    chain, width = lax.axis_size("tun"), lax.axis_size("sec")
    pairs_a = [(i, i ^ 1) for i in range(chain)]
    pairs_b = [(i, ((i + 1) ^ 1) - 1) for i in range(1, chain - 1)]
    msg_b, msg_a = pack_tun(onset, wind, heat, soot, mass, count, label)
    wind, heat, soot, mass, count, begins = load(onset, wind, heat, soot, mass, count, label, msg_b)
    got_b = lax.ppermute(msg_b, "tun", pairs_b)
    got_a = lax.ppermute(msg_a, "tun", pairs_a)
    to_low, to_high = pack_sec(wind, heat, soot, mass, count, begins, got_a, got_b)
    high = lax.ppermute(to_low, "sec", [(i + 1, i) for i in range(width - 1)])
    low = lax.ppermute(to_high, "sec", [(i, i + 1) for i in range(width - 1)])
    above = lax.ppermute(pack_mass(mass, to_low), "tun", [(i, i + 1) for i in range(chain - 1)])
    count_out, nxt, nxt_nu, keep, loads, spray_0, spray_1 = first(
        wind, heat, soot, mass, count, begins, got_a, got_b, to_low
    )
    wind_out, heat_out, soot_out, scale, gain, moved = last(
        high, low, to_low, to_high, count, got_a, got_b, loads, spray_0, spray_1, nxt, nxt_nu, keep
    )
    mass_out = droplets(mass, above, scale, gain, moved)
    return wind_out, heat_out, soot_out, mass_out, count_out


def solution(mesh):
    return jax.shard_map(
        local,
        mesh=mesh,
        in_specs=(
            P(None, "tun", "sec", None),
            P("tun", "sec", None),
            P("tun", "sec", None),
            P(None, "tun", "sec", None),
            P("tun", "sec", None),
            P("tun", "sec", None),
            P(),
        ),
        out_specs=(
            P(None, "tun", "sec", None),
            P("tun", "sec", None),
            P("tun", "sec", None),
            P(None, "tun", "sec", None),
            P("tun", "sec", None),
        ),
        check_vma=False,
    )
```

```python
import jax
import jax.numpy as jnp
from jax import lax
from jax.experimental import pallas as pl
from jax.experimental.pallas import tpu as pltpu
from jax.sharding import PartitionSpec as P

visc_base = 0.2
time_step = 0.1
buoyancy = 0.5
drag_rate = 0.3
vent_speed = 1.0
inject_rate = 0.5
evap_rate = 0.4
latent_heat = 0.5
scavenge = 0.3

NF = 5
F32 = jnp.float32
VMEM = pl.BlockSpec(memory_space=pltpu.VMEM)
SMEM = pl.BlockSpec(memory_space=pltpu.SMEM)
HBM = pl.BlockSpec(memory_space=pltpu.HBM)
ANY = pl.BlockSpec(memory_space=pl.ANY)
ROW = 8


FIRST_COST, LAST_COST = 0, 1


def cost(units):
    return pl.CostEstimate(flops=int(units * 1e9), transcendentals=0, bytes_accessed=int(units * 1e6))


LIMIT = pltpu.CompilerParams(vmem_limit_bytes=12 << 20)


def on_chip(*arrays):
    return tuple(pltpu.with_memory_space_constraint(a, pltpu.VMEM) for a in arrays)


def copies(pairs, sems):
    started = []
    for n, (src, dst) in enumerate(pairs):
        copy = pltpu.make_async_copy(src, dst, sems.at[n])
        copy.start()
        started.append(copy)
    return started

def live_sum(mass, count):
    total = jnp.zeros(count.shape, F32)
    for k in range(len(mass)):
        total = total + jnp.where(count > k, mass[k], 0.0)
    return total


def onset_of(label, onset):
    first = jnp.full(label.shape, 1 << 20, jnp.int32)
    for z in range(onset.shape[0]):
        first = jnp.where(label == z + 1, onset[z], first)
    return first


def pack_tun_kernel(
    onset, wind, heat, soot, mass, count, label, msg_b, msg_a, masses, counts, labels, onsets, sems
):
    depth = heat.shape[0]
    odd = lax.axis_index("tun") % 2 == 1
    top = depth - 2
    start_a = jnp.where(odd, 0, top)
    start_b = top - start_a
    pairs = [(onset, onsets), (mass.at[:, top:depth], masses), (count.at[top:depth], counts)]
    for n, (start, msg) in enumerate(((start_b, msg_b), (start_a, msg_a))):
        here = pl.ds(start, 2)
        pairs += [
            (label.at[here], labels.at[n]),
            (wind.at[:, here], msg.at[0:3]),
            (heat.at[here], msg.at[3]),
            (soot.at[here], msg.at[4]),
        ]
    for copy in copies(pairs, sems):
        copy.wait()
    held = counts[...]
    total = live_sum([masses[k] for k in range(masses.shape[0])], held)
    for n, msg in enumerate((msg_b, msg_a)):
        msg[NF] = onset_of(labels[n], onsets).astype(F32)
        msg[NF + 1] = held.astype(F32)
        msg[NF + 2] = total


def in_hbm(*arrays):
    return tuple(pltpu.with_memory_space_constraint(a, pltpu.HBM) for a in arrays)


def pack_tun(onset, wind, heat, soot, mass, count, label):
    plane = heat.shape[1:]
    msg = pltpu.VMEM((NF + 3, 2) + plane, F32)
    return pl.pallas_call(
        pack_tun_kernel,
        out_shape=(msg, msg),
        in_specs=[HBM] * 7,
        out_specs=(VMEM,) * 2,
        scratch_shapes=[
            pltpu.VMEM((mass.shape[0], 2) + plane, F32),
            pltpu.VMEM((2,) + plane, jnp.int32),
            pltpu.VMEM((2, 2) + plane, jnp.int32),
            pltpu.SMEM(onset.shape, jnp.int32),
            pltpu.SemaphoreType.DMA((11,)),
        ],
        compiler_params=LIMIT,
        name="pack_tun",
    )(*in_hbm(onset, wind, heat, soot, mass, count, label))


def load_kernel(onset, wind, heat, soot, mass, count, label, after, winds, heats, soots, masses, counts, begins, labels, onsets, sems):
    pairs = [
        (onset, onsets), (label, labels), (mass, masses), (wind, winds), (heat, heats), (soot, soots), (count, counts)
    ]
    pending = copies(pairs, sems)
    pending[0].wait()
    pending[1].wait()
    for x in range(label.shape[0]):
        begins[x] = onset_of(labels[x], onsets)
    for copy in pending[2:]:
        copy.wait()


def load(onset, wind, heat, soot, mass, count, label, after):
    arrays = (wind, heat, soot, mass, count, label)
    return pl.pallas_call(
        load_kernel,
        out_shape=tuple(pltpu.VMEM(a.shape, a.dtype) for a in arrays),
        in_specs=[HBM] * 7 + [ANY],
        out_specs=(VMEM,) * 6,
        scratch_shapes=[
            pltpu.VMEM(label.shape, jnp.int32),
            pltpu.SMEM(onset.shape, jnp.int32),
            pltpu.SemaphoreType.DMA((7,)),
        ],
        compiler_params=LIMIT,
        name="load",
    )(*in_hbm(onset, *arrays), after)


def pack_mass_kernel(mass, after, msg):
    depth = mass.shape[1]
    for k in range(mass.shape[0]):
        msg[k] = mass[k, depth - 2 : depth]


def pack_mass(mass, after):
    return pl.pallas_call(
        pack_mass_kernel,
        out_shape=pltpu.VMEM((mass.shape[0], 2) + mass.shape[2:], F32),
        in_specs=[VMEM] * 2,
        out_specs=VMEM,
        compiler_params=LIMIT,
        name="pack_mass",
    )(*on_chip(mass, after))


def pack_sec_kernel(got_b, got_a, wind, heat, soot, mass, count, begins, to_low, to_high, own_low, own_high):
    depth, rows, lanes = heat.shape
    slots = mass.shape[0]
    odd = lax.axis_index("tun") % 2 == 1

    def flat(ref):
        return ref.reshape(-1, lanes)

    winds, heats, soots, massed = flat(wind), flat(heat), flat(soot), flat(mass)
    counted, begun, from_a, from_b = flat(count), flat(begins), flat(got_a), flat(got_b)

    def own(f, row):
        ref, base = ((winds, f * depth * rows), (heats, 0), (soots, 0))[max(f - 2, 0)]
        return ref[pl.ds(base + row, depth, stride=rows), :]

    def beside(f, row):
        here = pl.ds(f * 2 * rows + row, 2, stride=rows)
        a, b = from_a[here, :], from_b[here, :]
        return jnp.where(odd, a, b), jnp.where(odd, b, a)

    for msg, kept, first, second in ((to_low, own_low, 0, 1), (to_high, own_high, rows - 1, rows - 2)):
        for f in range(NF):
            for n, row in ((f, first), (NF + f, second)):
                before, after = beside(f, row)
                centre = own(f, row)
                kept[n] = jnp.concatenate([before, centre, after], axis=0)
                msg[n] = centre
                if n < NF:
                    corner, place = 2 * NF + 1 + n // 4, 2 * (n % 4)
                    msg[corner, place : place + 2, :] = jnp.concatenate([before[1:], after[:1]], axis=0)
        here = pl.ds(first, depth, stride=rows)
        held = counted[here, :]
        sums = live_sum([massed[pl.ds(k * depth * rows + first, depth, stride=rows), :] for k in range(slots)], held)
        begins_up, begins_down = beside(NF, first)
        held_up, _ = beside(NF + 1, first)
        sums_up, _ = beside(NF + 2, first)
        starts = jnp.concatenate([begins_up[1:], begun[here, :].astype(F32), begins_down[:1]], axis=0)
        held = jnp.concatenate([held_up, held.astype(F32)], axis=0)
        sums = jnp.concatenate([sums_up, sums], axis=0)
        loads = sums + jnp.where(starts <= 0.0, inject_rate * held, 0.0)
        kept[2 * NF, 1 : 3 + depth, :] = loads
        msg[2 * NF] = loads[1 : 1 + depth]


def pack_sec(wind, heat, soot, mass, count, begins, got_a, got_b):
    depth, rows, lanes = heat.shape
    msg = pltpu.VMEM((2 * NF + 3, depth, lanes), F32)
    kept = pltpu.VMEM((2 * NF + 1, depth + 4, lanes), F32)
    return pl.pallas_call(
        pack_sec_kernel,
        out_shape=(msg, msg, kept, kept),
        in_specs=[VMEM] * 8,
        out_specs=(VMEM,) * 4,
        compiler_params=LIMIT,
        name="pack_sec",
    )(*on_chip(got_b, got_a, wind, heat, soot, mass, count, begins))


def viscosity(heat):
    return visc_base * (1.0 + 0.5 * jnp.tanh(heat))


def stencil(centre, nu, sides, nu_sides):
    lane = lax.broadcasted_iota(jnp.int32, nu.shape, 1)
    last = nu.shape[1] - 1
    rest = None
    weights = []
    for d in range(3):
        for side, sign in ((0, -1.0), (1, 1.0)):
            weight = (0.5 * time_step) * ((nu + nu_sides[d][side]) - sign * centre[d])
            rest = weight if rest is None else rest + weight
            if d == 2:
                weight = jnp.where(lane == (last if side else 0), 0.0, weight)
            weights.append(weight)
    rest = 1.0 - rest
    out = []
    for f in range(NF):
        value = rest * centre[f]
        for d in range(3):
            for side in (0, 1):
                value = value + weights[2 * d + side] * sides[d][side](f)
        out.append(value)
    out[0] = out[0] + (time_step * drag_rate) * (vent_speed - centre[0])
    out[2] = out[2] + (time_step * buoyancy) * centre[3]
    return out


def around(plane):
    return pltpu.roll(plane, 1, 1), pltpu.roll(plane, plane.shape[1] - 1, 1)


def nu_around(nu):
    lane = lax.broadcasted_iota(jnp.int32, nu.shape, 1)
    low, high = around(nu)
    return jnp.where(lane == 0, visc_base, low), jnp.where(lane == nu.shape[1] - 1, visc_base, high)


def first_kernel(
    wind, heat, soot, mass, count, begins, got_a, got_b, after,
    count_out, nxt, nxt_nu, keep, loads, spray_0, spray_1,
    ext, ext_nu, counts, sems,
):
    depth, rows, lanes = heat.shape
    slots = mass.shape[0]
    tall = rows + 2 * ROW
    tun = lax.axis_index("tun")
    odd = tun % 2 == 1
    own = [wind.at[0], wind.at[1], wind.at[2], heat, soot]

    def beside(n, x):
        return jnp.where(odd, got_a[n, x], got_b[n, x]), jnp.where(odd, got_b[n, x], got_a[n, x])

    def put(ref, plane, value):
        ref[plane * tall + ROW : plane * tall + ROW + rows, :] = value

    def at(ref, plane, shift=0):
        return ref[plane * tall + ROW + shift : plane * tall + ROW + shift + rows, :]

    planes = depth + 4
    for f in range(NF):
        for x in range(depth):
            put(ext, f * planes + x + 2, own[f][x])
        for x in (0, 1):
            before, behind = beside(f, x)
            put(ext, f * planes + x, before)
            put(ext, f * planes + depth + 2 + x, behind)
    for x in range(planes):
        put(ext_nu, x, viscosity(at(ext, 3 * planes + x)))

    for x in (0, 1):
        counts[x] = beside(NF + 1, x)[0].astype(jnp.int32)
    for x in range(depth - 2):
        counts[x + 2] = count[x]
    pending = copies([(counts, count_out)], sems)

    for x in range(-1, depth + 1):
        centre = [at(ext, f * planes + x + 2) for f in range(NF)]
        nu = at(ext_nu, x + 2)
        lifted = [around(c) for c in centre]
        sides = [
            (lambda f: at(ext, f * planes + x + 1), lambda f: at(ext, f * planes + x + 3)),
            (lambda f: at(ext, f * planes + x + 2, -1), lambda f: at(ext, f * planes + x + 2, 1)),
            (lambda f: lifted[f][0], lambda f: lifted[f][1]),
        ]
        nu_sides = [
            (at(ext_nu, x + 1), at(ext_nu, x + 3)),
            (at(ext_nu, x + 2, -1), at(ext_nu, x + 2, 1)),
            nu_around(nu),
        ]
        new = stencil(centre, nu, sides, nu_sides)
        if x < 1:
            moved_total, moved_count = beside(NF + 2, x + 1)[0], beside(NF + 1, x + 1)[0]
        else:
            held = count[x - 1]
            moved_total, moved_count = live_sum([mass[k, x - 1] for k in range(slots)], held), held.astype(F32)
        if x < 0:
            start = beside(NF, 1)[0].astype(jnp.int32)
        elif x < depth:
            start = begins[x]
        else:
            start = beside(NF, 0)[1].astype(jnp.int32)
        sprays = jnp.where(start <= 0, inject_rate, 0.0)
        load = moved_total + sprays * moved_count
        evap = evap_rate * jax.nn.sigmoid(new[3])
        new[3] = new[3] - latent_heat * (evap * load)
        new[4] = new[4] / (1.0 + scavenge * load)
        if x < depth:
            keep[(x + 1) * rows : (x + 2) * rows, :] = 1.0 - evap
            loads[x + 1] = load
            spray_0[x + 1] = sprays
        if 0 <= x < depth:
            spray_1[x] = jnp.where(start <= 1, inject_rate, 0.0)
        inside = tun > 0 if x < 0 else tun < lax.axis_size("tun") - 1 if x == depth else None
        for f in range(NF):
            value = new[f] if inside is None else jnp.where(inside, new[f], 0.0)
            put(nxt, f * (depth + 2) + x + 1, value)
            if f == 3:
                put(nxt_nu, x + 1, viscosity(value))
    for copy in pending:
        copy.wait()


def first(wind, heat, soot, mass, count, begins, got_a, got_b, after):
    depth, rows, lanes = heat.shape
    tall = rows + 2 * ROW
    return pl.pallas_call(
        first_kernel,
        out_shape=(
            jax.ShapeDtypeStruct(count.shape, jnp.int32),
            pltpu.VMEM((NF * (depth + 2) * tall, lanes), F32),
            pltpu.VMEM(((depth + 2) * tall, lanes), F32),
            pltpu.VMEM(((depth + 1) * rows, lanes), F32),
            pltpu.VMEM((depth + 1, rows, lanes), F32),
            pltpu.VMEM((depth + 1, rows, lanes), F32),
            pltpu.VMEM((depth, rows, lanes), F32),
        ),
        in_specs=[VMEM] * 8 + [ANY],
        out_specs=(ANY,) + (VMEM,) * 6,
        scratch_shapes=[
            pltpu.VMEM((NF * (depth + 4) * tall, lanes), F32),
            pltpu.VMEM(((depth + 4) * tall, lanes), F32),
            pltpu.VMEM((depth, rows, lanes), jnp.int32),
            pltpu.SemaphoreType.DMA((1,)),
        ],
        compiler_params=LIMIT,
        cost_estimate=cost(FIRST_COST),
        name="first_substep",
    )(*on_chip(wind, heat, soot, mass, count, begins, got_a, got_b), after)


def last_kernel(
    high, low, own_low, own_high, count, got_a, got_b, loads, spray_0, spray_1, nxt_in, nxt_nu_in, keep_in,
    wind_out, heat_out, soot_out, scale, gain, moved, nxt, nxt_nu, keep,
    fields, beside, sems,
):
    depth, rows, lanes = count.shape
    tall = rows + 2 * ROW
    planes = depth + 2
    tun, sec = lax.axis_index("tun"), lax.axis_index("sec")
    odd = tun % 2 == 1
    inside_up, inside_down = tun > 0, tun < lax.axis_size("tun") - 1
    place = lax.broadcasted_iota(jnp.int32, (planes, lanes), 0)
    inside = ((place > 0) | inside_up) & ((place < planes - 1) | inside_down)

    def step(centre, nu, sides, nu_sides, load):
        new = stencil(centre, nu, sides, nu_sides)
        evap = evap_rate * jax.nn.sigmoid(new[3])
        new[3] = new[3] - latent_heat * (evap * load)
        new[4] = new[4] / (1.0 + scavenge * load)
        return new, 1.0 - evap

    for flip, (got, own, outer_row, inner_row, there) in enumerate(
        (
            (low, own_low, ROW - 1, 0, sec > 0),
            (high, own_high, ROW + rows, rows - 1, sec < lax.axis_size("sec") - 1),
        )
    ):
        line = beside.at[flip]
        for f in range(NF):
            corner, spot = 2 * NF + 1 + f // 4, 2 * (f % 4)
            line[f, 8 : 8 + depth, :] = got[f]
            line[f, 7:8, :] = got[corner, spot : spot + 1, :]
            line[f, 8 + depth : 9 + depth, :] = got[corner, spot + 1 : spot + 2, :]
        wide, block = slice(7, 9 + depth), slice(8, 8 + depth)
        line_nu, own_nu = viscosity(line[3, wide, :]), viscosity(own[3])

        def ordered(near, far, swap):
            return (near, far) if swap else (far, near)

        centre = [line[f, block, :] for f in range(NF)]
        lifted = [around(c) for c in centre]
        nu = line_nu[1 : 1 + depth]
        new, _ = step(
            centre,
            nu,
            [
                (lambda f: line[f, 7 : 7 + depth, :], lambda f: line[f, 9 : 9 + depth, :]),
                ordered(lambda f: own[f, 2 : 2 + depth, :], lambda f: got[NF + f], flip == 1),
                (lambda f: lifted[f][0], lambda f: lifted[f][1]),
            ],
            [
                (line_nu[0:depth], line_nu[2 : 2 + depth]),
                ordered(own_nu[2 : 2 + depth], viscosity(got[NF + 3]), flip == 1),
                nu_around(nu),
            ],
            got[2 * NF],
        )
        for f in range(NF):
            value = jnp.where(there, new[f], 0.0)
            nxt[pl.ds((f * planes + 1) * tall + outer_row, depth, stride=tall), :] = value
            if f == 3:
                nxt_nu[pl.ds(tall + outer_row, depth, stride=tall), :] = viscosity(value)

        mid = slice(1, 1 + planes)
        centre = [own[f, mid, :] for f in range(NF)]
        lifted = [around(c) for c in centre]
        nu = own_nu[mid]
        new, left = step(
            centre,
            nu,
            [
                (lambda f: own[f, 0:planes, :], lambda f: own[f, 2 : 2 + planes, :]),
                ordered(lambda f: line[f, wide, :], lambda f: own[NF + f, mid, :], flip == 0),
                (lambda f: lifted[f][0], lambda f: lifted[f][1]),
            ],
            [
                (own_nu[0:planes], own_nu[2 : 2 + planes]),
                ordered(line_nu, viscosity(own[NF + 3, mid, :]), flip == 0),
                nu_around(nu),
            ],
            own[2 * NF, mid, :],
        )
        for f in range(NF):
            value = jnp.where(inside, new[f], 0.0)
            nxt[pl.ds(f * planes * tall + ROW + inner_row, planes, stride=tall), :] = value
            if f == 3:
                nxt_nu[pl.ds(ROW + inner_row, planes, stride=tall), :] = viscosity(value)
        keep[pl.ds(inner_row, depth + 1, stride=rows), :] = left[: depth + 1]

    def at(ref, plane, shift=0):
        return ref[plane * tall + ROW + shift : plane * tall + ROW + shift + rows, :]

    for x in range(depth):
        centre = [at(nxt, f * planes + x + 1) for f in range(NF)]
        nu = at(nxt_nu, x + 1)
        lifted = [around(c) for c in centre]
        sides = [
            (lambda f: at(nxt, f * planes + x), lambda f: at(nxt, f * planes + x + 2)),
            (lambda f: at(nxt, f * planes + x + 1, -1), lambda f: at(nxt, f * planes + x + 1, 1)),
            (lambda f: lifted[f][0], lambda f: lifted[f][1]),
        ]
        nu_sides = [
            (at(nxt_nu, x), at(nxt_nu, x + 2)),
            (at(nxt_nu, x + 1, -1), at(nxt_nu, x + 1, 1)),
            nu_around(nu),
        ]
        new = stencil(centre, nu, sides, nu_sides)
        if x < 2:
            held = jnp.where(odd, got_a[NF + 1, x], got_b[NF + 1, x]).astype(jnp.int32)
        else:
            held = count[x - 2]
        kept = keep[x * rows : (x + 1) * rows, :]
        sprays = spray_1[x]
        load = loads[x] * kept + sprays * held.astype(F32)
        evap = evap_rate * jax.nn.sigmoid(new[3])
        new[3] = new[3] - latent_heat * (evap * load)
        new[4] = new[4] / (1.0 + scavenge * load)
        for f in range(NF):
            fields[f, x] = new[f]
        moved[x] = held
        scale[x] = kept * (1.0 - evap)
        gain[x] = (spray_0[x] * kept + sprays) * (1.0 - evap)
    for copy in copies([(fields.at[0:3], wind_out), (fields.at[3], heat_out), (fields.at[4], soot_out)], sems):
        copy.wait()


def last(high, low, own_low, own_high, count, got_a, got_b, loads, spray_0, spray_1, nxt, nxt_nu, keep):
    block = count.shape
    operands = on_chip(high, low, own_low, own_high, count, got_a, got_b, loads, spray_0, spray_1, nxt, nxt_nu, keep)
    return pl.pallas_call(
        last_kernel,
        out_shape=(
            jax.ShapeDtypeStruct((3,) + block, F32),
            jax.ShapeDtypeStruct(block, F32),
            jax.ShapeDtypeStruct(block, F32),
            pltpu.VMEM(block, F32),
            pltpu.VMEM(block, F32),
            pltpu.VMEM(block, jnp.int32),
            pltpu.VMEM(nxt.shape, F32),
            pltpu.VMEM(nxt_nu.shape, F32),
            pltpu.VMEM(keep.shape, F32),
        ),
        in_specs=[VMEM] * 13,
        out_specs=(ANY,) * 3 + (VMEM,) * 6,
        input_output_aliases={10: 6, 11: 7, 12: 8},
        scratch_shapes=[
            pltpu.VMEM((NF,) + block, F32),
            pltpu.VMEM((2, NF, block[0] + 16, block[2]), F32),
            pltpu.SemaphoreType.DMA((3,)),
        ],
        compiler_params=LIMIT,
        cost_estimate=cost(LAST_COST),
        name="last_substep",
    )(*operands)[:6]


def droplets_kernel(mass, above, scale, gain, moved, mass_out, masses, sems):
    slots, depth = mass.shape[:2]
    pending = []
    for x in range(depth):
        held, by, plus = moved[x], scale[x], gain[x]
        for k in range(slots):
            before = above[k, x] if x < 2 else mass[k, x - 2]
            masses[k, x] = jnp.where(held > k, before * by + plus, before)
        copy = pltpu.make_async_copy(masses.at[:, x], mass_out.at[:, x], sems.at[x])
        copy.start()
        pending.append(copy)
    for copy in pending:
        copy.wait()


def droplets(mass, above, scale, gain, moved):
    return pl.pallas_call(
        droplets_kernel,
        out_shape=jax.ShapeDtypeStruct(mass.shape, F32),
        in_specs=[VMEM] * 5,
        out_specs=ANY,
        scratch_shapes=[pltpu.VMEM(mass.shape, F32), pltpu.SemaphoreType.DMA((mass.shape[1],))],
        compiler_params=LIMIT,
        name="droplets",
    )(*on_chip(mass, above, scale, gain, moved))


def local(wind, heat, soot, mass, count, label, onset):
    chain, width = lax.axis_size("tun"), lax.axis_size("sec")
    pairs_a = [(i, i ^ 1) for i in range(chain)]
    pairs_b = [(i, ((i + 1) ^ 1) - 1) for i in range(1, chain - 1)]
    msg_b, msg_a = pack_tun(onset, wind, heat, soot, mass, count, label)
    wind, heat, soot, mass, count, begins = load(onset, wind, heat, soot, mass, count, label, msg_b)
    got_b = lax.ppermute(msg_b, "tun", pairs_b)
    got_a = lax.ppermute(msg_a, "tun", pairs_a)
    to_low, to_high, own_low, own_high = pack_sec(wind, heat, soot, mass, count, begins, got_a, got_b)
    high = lax.ppermute(to_low, "sec", [(i + 1, i) for i in range(width - 1)])
    low = lax.ppermute(to_high, "sec", [(i, i + 1) for i in range(width - 1)])
    above = lax.ppermute(pack_mass(mass, got_b), "tun", [(i, i + 1) for i in range(chain - 1)])
    count_out, nxt, nxt_nu, keep, loads, spray_0, spray_1 = first(
        wind, heat, soot, mass, count, begins, got_a, got_b, to_low
    )
    wind_out, heat_out, soot_out, scale, gain, moved = last(
        high, low, own_low, own_high, count, got_a, got_b, loads, spray_0, spray_1, nxt, nxt_nu, keep
    )
    mass_out = droplets(mass, above, scale, gain, moved)
    return wind_out, heat_out, soot_out, mass_out, count_out


def solution(mesh):
    return jax.shard_map(
        local,
        mesh=mesh,
        in_specs=(
            P(None, "tun", "sec", None),
            P("tun", "sec", None),
            P("tun", "sec", None),
            P(None, "tun", "sec", None),
            P("tun", "sec", None),
            P("tun", "sec", None),
            P(),
        ),
        out_specs=(
            P(None, "tun", "sec", None),
            P("tun", "sec", None),
            P("tun", "sec", None),
            P(None, "tun", "sec", None),
            P("tun", "sec", None),
        ),
        check_vma=False,
    )
```

```python
import jax
import jax.numpy as jnp
from jax import lax
from jax.experimental import pallas as pl
from jax.experimental.pallas import tpu as pltpu
from jax.sharding import PartitionSpec as P

visc_base = 0.2
time_step = 0.1
buoyancy = 0.5
drag_rate = 0.3
vent_speed = 1.0
inject_rate = 0.5
evap_rate = 0.4
latent_heat = 0.5
scavenge = 0.3

NF = 5
F32 = jnp.float32
VMEM = pl.BlockSpec(memory_space=pltpu.VMEM)
SMEM = pl.BlockSpec(memory_space=pltpu.SMEM)
HBM = pl.BlockSpec(memory_space=pltpu.HBM)
ANY = pl.BlockSpec(memory_space=pl.ANY)
ROW = 8


FIRST_COST, LAST_COST = 0, 1


def cost(units):
    return pl.CostEstimate(flops=int(units * 1e9), transcendentals=0, bytes_accessed=int(units * 1e6))


LIMIT = pltpu.CompilerParams(vmem_limit_bytes=12 << 20)


def on_chip(*arrays):
    return tuple(pltpu.with_memory_space_constraint(a, pltpu.VMEM) for a in arrays)


def copies(pairs, sems):
    started = []
    for n, (src, dst) in enumerate(pairs):
        copy = pltpu.make_async_copy(src, dst, sems.at[n])
        copy.start()
        started.append(copy)
    return started

def live_sum(mass, count):
    total = jnp.zeros(count.shape, F32)
    for k in range(len(mass)):
        total = total + jnp.where(count > k, mass[k], 0.0)
    return total


def onset_of(label, onset):
    first = jnp.full(label.shape, 1 << 20, jnp.int32)
    for z in range(onset.shape[0]):
        first = jnp.where(label == z + 1, onset[z], first)
    return first


def pack_tun_kernel(
    onset, wind, heat, soot, mass, count, label,
    msg_b, msg_a, winds, heats, soots, masses, counts, begins, labels, onsets, sems,
):
    depth = heat.shape[0]
    odd = lax.axis_index("tun") % 2 == 1
    top = depth - 2
    start_a = jnp.where(odd, 0, top)
    start_b = top - start_a
    onset_copy, label_copy, count_copy, *others = copies(
        [
            (onset, onsets), (label, labels), (count, counts), (mass, masses), (wind, winds), (heat, heats), (soot, soots)
        ],
        sems,
    )
    onset_copy.wait()
    label_copy.wait()
    for x in range(depth):
        begins[x] = onset_of(labels[x], onsets)
    count_copy.wait()
    others[0].wait()
    held = counts[top:depth]
    total = live_sum([masses[k, top:depth] for k in range(masses.shape[0])], held)
    for copy in others[1:]:
        copy.wait()
    for start, msg in ((start_b, msg_b), (start_a, msg_a)):
        here = pl.ds(start, 2)
        for f in range(3):
            msg[f] = winds[f, here]
        msg[3] = heats[here]
        msg[4] = soots[here]
        msg[NF] = begins[here].astype(F32)
        msg[NF + 1] = held.astype(F32)
        msg[NF + 2] = total


def in_hbm(*arrays):
    return tuple(pltpu.with_memory_space_constraint(a, pltpu.HBM) for a in arrays)


def pack_tun(onset, wind, heat, soot, mass, count, label):
    arrays = (wind, heat, soot, mass, count, label)
    msg = pltpu.VMEM((NF + 3, 2) + heat.shape[1:], F32)
    return pl.pallas_call(
        pack_tun_kernel,
        out_shape=(msg, msg) + tuple(pltpu.VMEM(a.shape, a.dtype) for a in arrays),
        in_specs=[HBM] * 7,
        out_specs=(VMEM,) * 8,
        scratch_shapes=[
            pltpu.VMEM(label.shape, jnp.int32),
            pltpu.SMEM(onset.shape, jnp.int32),
            pltpu.SemaphoreType.DMA((7,)),
        ],
        compiler_params=LIMIT,
        name="pack_tun",
    )(*in_hbm(onset, *arrays))


def pack_mass_kernel(mass, after, msg):
    depth = mass.shape[1]
    for k in range(mass.shape[0]):
        msg[k] = mass[k, depth - 2 : depth]


def pack_mass(mass, after):
    return pl.pallas_call(
        pack_mass_kernel,
        out_shape=pltpu.VMEM((mass.shape[0], 2) + mass.shape[2:], F32),
        in_specs=[VMEM] * 2,
        out_specs=VMEM,
        compiler_params=LIMIT,
        name="pack_mass",
    )(*on_chip(mass, after))


def pack_sec_kernel(got_b, got_a, wind, heat, soot, mass, count, begins, msg_x, msg_y, own_low, own_high, to_low, to_high):
    depth, rows, lanes = heat.shape
    slots = mass.shape[0]
    odd = lax.axis_index("tun") % 2 == 1

    def flat(ref):
        return ref.reshape(-1, lanes)

    winds, heats, soots, massed = flat(wind), flat(heat), flat(soot), flat(mass)
    counted, begun, from_a, from_b = flat(count), flat(begins), flat(got_a), flat(got_b)

    def own(f, row):
        ref, base = ((winds, f * depth * rows), (heats, 0), (soots, 0))[max(f - 2, 0)]
        return ref[pl.ds(base + row, depth, stride=rows), :]

    def beside(f, row):
        here = pl.ds(f * 2 * rows + row, 2, stride=rows)
        a, b = from_a[here, :], from_b[here, :]
        return jnp.where(odd, a, b), jnp.where(odd, b, a)

    for msg, kept, first, second in ((to_low, own_low, 0, 1), (to_high, own_high, rows - 1, rows - 2)):
        for f in range(NF):
            for n, row in ((f, first), (NF + f, second)):
                before, after = beside(f, row)
                centre = own(f, row)
                kept[n] = jnp.concatenate([before, centre, after], axis=0)
                msg[n] = centre
                if n < NF:
                    corner, place = 2 * NF + 1 + n // 4, 2 * (n % 4)
                    msg[corner, place : place + 2, :] = jnp.concatenate([before[1:], after[:1]], axis=0)
        here = pl.ds(first, depth, stride=rows)
        held = counted[here, :]
        sums = live_sum([massed[pl.ds(k * depth * rows + first, depth, stride=rows), :] for k in range(slots)], held)
        begins_up, begins_down = beside(NF, first)
        held_up, _ = beside(NF + 1, first)
        sums_up, _ = beside(NF + 2, first)
        starts = jnp.concatenate([begins_up[1:], begun[here, :].astype(F32), begins_down[:1]], axis=0)
        held = jnp.concatenate([held_up, held.astype(F32)], axis=0)
        sums = jnp.concatenate([sums_up, sums], axis=0)
        loads = sums + jnp.where(starts <= 0.0, inject_rate * held, 0.0)
        kept[2 * NF, 1 : 3 + depth, :] = loads
        msg[2 * NF] = loads[1 : 1 + depth]
    odd_row = lax.axis_index("sec") % 2 == 1
    for n in range(2 * NF + 3):
        lower, upper = to_low[n], to_high[n]
        msg_x[n] = jnp.where(odd_row, lower, upper)
        msg_y[n] = jnp.where(odd_row, upper, lower)


def pack_sec(wind, heat, soot, mass, count, begins, got_a, got_b):
    depth, rows, lanes = heat.shape
    msg = pltpu.VMEM((2 * NF + 3, depth, lanes), F32)
    kept = pltpu.VMEM((2 * NF + 1, depth + 4, lanes), F32)
    return pl.pallas_call(
        pack_sec_kernel,
        out_shape=(msg, msg, kept, kept),
        in_specs=[VMEM] * 8,
        out_specs=(VMEM,) * 4,
        scratch_shapes=[pltpu.VMEM((2 * NF + 3, depth, lanes), F32)] * 2,
        compiler_params=LIMIT,
        name="pack_sec",
    )(*on_chip(got_b, got_a, wind, heat, soot, mass, count, begins))


def viscosity(heat):
    return visc_base * (1.0 + 0.5 * jnp.tanh(heat))


def stencil(centre, nu, sides, nu_sides):
    lane = lax.broadcasted_iota(jnp.int32, nu.shape, 1)
    last = nu.shape[1] - 1
    rest = None
    weights = []
    for d in range(3):
        for side, sign in ((0, -1.0), (1, 1.0)):
            weight = (0.5 * time_step) * ((nu + nu_sides[d][side]) - sign * centre[d])
            rest = weight if rest is None else rest + weight
            if d == 2:
                weight = jnp.where(lane == (last if side else 0), 0.0, weight)
            weights.append(weight)
    rest = 1.0 - rest
    out = []
    for f in range(NF):
        value = rest * centre[f]
        for d in range(3):
            for side in (0, 1):
                value = value + weights[2 * d + side] * sides[d][side](f)
        out.append(value)
    out[0] = out[0] + (time_step * drag_rate) * (vent_speed - centre[0])
    out[2] = out[2] + (time_step * buoyancy) * centre[3]
    return out


def around(plane):
    return pltpu.roll(plane, 1, 1), pltpu.roll(plane, plane.shape[1] - 1, 1)


def nu_around(nu):
    lane = lax.broadcasted_iota(jnp.int32, nu.shape, 1)
    low, high = around(nu)
    return jnp.where(lane == 0, visc_base, low), jnp.where(lane == nu.shape[1] - 1, visc_base, high)


def first_kernel(
    wind, heat, soot, mass, count, begins, got_a, got_b, after,
    count_out, nxt, nxt_nu, keep, loads, spray_0, spray_1,
    ext, ext_nu, counts, sems,
):
    depth, rows, lanes = heat.shape
    slots = mass.shape[0]
    tall = rows + 2 * ROW
    tun = lax.axis_index("tun")
    odd = tun % 2 == 1
    own = [wind.at[0], wind.at[1], wind.at[2], heat, soot]

    def beside(n, x):
        return jnp.where(odd, got_a[n, x], got_b[n, x]), jnp.where(odd, got_b[n, x], got_a[n, x])

    def put(ref, plane, value):
        ref[plane * tall + ROW : plane * tall + ROW + rows, :] = value

    def at(ref, plane, shift=0):
        return ref[plane * tall + ROW + shift : plane * tall + ROW + shift + rows, :]

    planes = depth + 4
    for f in range(NF):
        for x in range(depth):
            put(ext, f * planes + x + 2, own[f][x])
        for x in (0, 1):
            before, behind = beside(f, x)
            put(ext, f * planes + x, before)
            put(ext, f * planes + depth + 2 + x, behind)
    for x in range(planes):
        put(ext_nu, x, viscosity(at(ext, 3 * planes + x)))

    for x in (0, 1):
        counts[x] = beside(NF + 1, x)[0].astype(jnp.int32)
    for x in range(depth - 2):
        counts[x + 2] = count[x]
    pending = copies([(counts, count_out)], sems)

    for x in range(-1, depth + 1):
        centre = [at(ext, f * planes + x + 2) for f in range(NF)]
        nu = at(ext_nu, x + 2)
        lifted = [around(c) for c in centre]
        sides = [
            (lambda f: at(ext, f * planes + x + 1), lambda f: at(ext, f * planes + x + 3)),
            (lambda f: at(ext, f * planes + x + 2, -1), lambda f: at(ext, f * planes + x + 2, 1)),
            (lambda f: lifted[f][0], lambda f: lifted[f][1]),
        ]
        nu_sides = [
            (at(ext_nu, x + 1), at(ext_nu, x + 3)),
            (at(ext_nu, x + 2, -1), at(ext_nu, x + 2, 1)),
            nu_around(nu),
        ]
        new = stencil(centre, nu, sides, nu_sides)
        if x < 1:
            moved_total, moved_count = beside(NF + 2, x + 1)[0], beside(NF + 1, x + 1)[0]
        else:
            held = count[x - 1]
            moved_total, moved_count = live_sum([mass[k, x - 1] for k in range(slots)], held), held.astype(F32)
        if x < 0:
            start = beside(NF, 1)[0].astype(jnp.int32)
        elif x < depth:
            start = begins[x]
        else:
            start = beside(NF, 0)[1].astype(jnp.int32)
        sprays = jnp.where(start <= 0, inject_rate, 0.0)
        load = moved_total + sprays * moved_count
        evap = evap_rate * jax.nn.sigmoid(new[3])
        new[3] = new[3] - latent_heat * (evap * load)
        new[4] = new[4] / (1.0 + scavenge * load)
        if x < depth:
            keep[(x + 1) * rows : (x + 2) * rows, :] = 1.0 - evap
            loads[x + 1] = load
            spray_0[x + 1] = sprays
        if 0 <= x < depth:
            spray_1[x] = jnp.where(start <= 1, inject_rate, 0.0)
        inside = tun > 0 if x < 0 else tun < lax.axis_size("tun") - 1 if x == depth else None
        for f in range(NF):
            value = new[f] if inside is None else jnp.where(inside, new[f], 0.0)
            put(nxt, f * (depth + 2) + x + 1, value)
            if f == 3:
                put(nxt_nu, x + 1, viscosity(value))
    for copy in pending:
        copy.wait()


def first(wind, heat, soot, mass, count, begins, got_a, got_b, after):
    depth, rows, lanes = heat.shape
    tall = rows + 2 * ROW
    return pl.pallas_call(
        first_kernel,
        out_shape=(
            jax.ShapeDtypeStruct(count.shape, jnp.int32),
            pltpu.VMEM((NF * (depth + 2) * tall, lanes), F32),
            pltpu.VMEM(((depth + 2) * tall, lanes), F32),
            pltpu.VMEM(((depth + 1) * rows, lanes), F32),
            pltpu.VMEM((depth + 1, rows, lanes), F32),
            pltpu.VMEM((depth + 1, rows, lanes), F32),
            pltpu.VMEM((depth, rows, lanes), F32),
        ),
        in_specs=[VMEM] * 8 + [ANY],
        out_specs=(ANY,) + (VMEM,) * 6,
        scratch_shapes=[
            pltpu.VMEM((NF * (depth + 4) * tall, lanes), F32),
            pltpu.VMEM(((depth + 4) * tall, lanes), F32),
            pltpu.VMEM((depth, rows, lanes), jnp.int32),
            pltpu.SemaphoreType.DMA((1,)),
        ],
        compiler_params=LIMIT,
        cost_estimate=cost(FIRST_COST),
        name="first_substep",
    )(*on_chip(wind, heat, soot, mass, count, begins, got_a, got_b), after)


def last_kernel(
    got_x, got_y, own_low, own_high, count, got_a, got_b, loads, spray_0, spray_1, nxt_in, nxt_nu_in, keep_in,
    fields, scale, gain, moved, nxt, nxt_nu, keep,
    beside, low, high,
):
    depth, rows, lanes = count.shape
    tall = rows + 2 * ROW
    planes = depth + 2
    tun, sec = lax.axis_index("tun"), lax.axis_index("sec")
    odd = tun % 2 == 1
    inside_up, inside_down = tun > 0, tun < lax.axis_size("tun") - 1
    odd_row = sec % 2 == 1
    for n in range(2 * NF + 3):
        x, y = got_x[n], got_y[n]
        low[n] = jnp.where(odd_row, x, y)
        high[n] = jnp.where(odd_row, y, x)

    place = lax.broadcasted_iota(jnp.int32, (planes, lanes), 0)
    inside = ((place > 0) | inside_up) & ((place < planes - 1) | inside_down)

    def step(centre, nu, sides, nu_sides, load):
        new = stencil(centre, nu, sides, nu_sides)
        evap = evap_rate * jax.nn.sigmoid(new[3])
        new[3] = new[3] - latent_heat * (evap * load)
        new[4] = new[4] / (1.0 + scavenge * load)
        return new, 1.0 - evap

    for flip, (got, own, outer_row, inner_row, there) in enumerate(
        (
            (low, own_low, ROW - 1, 0, sec > 0),
            (high, own_high, ROW + rows, rows - 1, sec < lax.axis_size("sec") - 1),
        )
    ):
        line = beside.at[flip]
        for f in range(NF):
            corner, spot = 2 * NF + 1 + f // 4, 2 * (f % 4)
            line[f, 8 : 8 + depth, :] = got[f]
            line[f, 7:8, :] = got[corner, spot : spot + 1, :]
            line[f, 8 + depth : 9 + depth, :] = got[corner, spot + 1 : spot + 2, :]
        wide, block = slice(7, 9 + depth), slice(8, 8 + depth)
        line_nu, own_nu = viscosity(line[3, wide, :]), viscosity(own[3])

        def ordered(near, far, swap):
            return (near, far) if swap else (far, near)

        centre = [line[f, block, :] for f in range(NF)]
        lifted = [around(c) for c in centre]
        nu = line_nu[1 : 1 + depth]
        new, _ = step(
            centre,
            nu,
            [
                (lambda f: line[f, 7 : 7 + depth, :], lambda f: line[f, 9 : 9 + depth, :]),
                ordered(lambda f: own[f, 2 : 2 + depth, :], lambda f: got[NF + f], flip == 1),
                (lambda f: lifted[f][0], lambda f: lifted[f][1]),
            ],
            [
                (line_nu[0:depth], line_nu[2 : 2 + depth]),
                ordered(own_nu[2 : 2 + depth], viscosity(got[NF + 3]), flip == 1),
                nu_around(nu),
            ],
            got[2 * NF],
        )
        for f in range(NF):
            value = jnp.where(there, new[f], 0.0)
            nxt[pl.ds((f * planes + 1) * tall + outer_row, depth, stride=tall), :] = value
            if f == 3:
                nxt_nu[pl.ds(tall + outer_row, depth, stride=tall), :] = viscosity(value)

        mid = slice(1, 1 + planes)
        centre = [own[f, mid, :] for f in range(NF)]
        lifted = [around(c) for c in centre]
        nu = own_nu[mid]
        new, left = step(
            centre,
            nu,
            [
                (lambda f: own[f, 0:planes, :], lambda f: own[f, 2 : 2 + planes, :]),
                ordered(lambda f: line[f, wide, :], lambda f: own[NF + f, mid, :], flip == 0),
                (lambda f: lifted[f][0], lambda f: lifted[f][1]),
            ],
            [
                (own_nu[0:planes], own_nu[2 : 2 + planes]),
                ordered(line_nu, viscosity(own[NF + 3, mid, :]), flip == 0),
                nu_around(nu),
            ],
            own[2 * NF, mid, :],
        )
        for f in range(NF):
            value = jnp.where(inside, new[f], 0.0)
            nxt[pl.ds(f * planes * tall + ROW + inner_row, planes, stride=tall), :] = value
            if f == 3:
                nxt_nu[pl.ds(ROW + inner_row, planes, stride=tall), :] = viscosity(value)
        keep[pl.ds(inner_row, depth + 1, stride=rows), :] = left[: depth + 1]

    def at(ref, plane, shift=0):
        return ref[plane * tall + ROW + shift : plane * tall + ROW + shift + rows, :]

    for x in range(depth):
        centre = [at(nxt, f * planes + x + 1) for f in range(NF)]
        nu = at(nxt_nu, x + 1)
        lifted = [around(c) for c in centre]
        sides = [
            (lambda f: at(nxt, f * planes + x), lambda f: at(nxt, f * planes + x + 2)),
            (lambda f: at(nxt, f * planes + x + 1, -1), lambda f: at(nxt, f * planes + x + 1, 1)),
            (lambda f: lifted[f][0], lambda f: lifted[f][1]),
        ]
        nu_sides = [
            (at(nxt_nu, x), at(nxt_nu, x + 2)),
            (at(nxt_nu, x + 1, -1), at(nxt_nu, x + 1, 1)),
            nu_around(nu),
        ]
        new = stencil(centre, nu, sides, nu_sides)
        if x < 2:
            held = jnp.where(odd, got_a[NF + 1, x], got_b[NF + 1, x]).astype(jnp.int32)
        else:
            held = count[x - 2]
        kept = keep[x * rows : (x + 1) * rows, :]
        sprays = spray_1[x]
        load = loads[x] * kept + sprays * held.astype(F32)
        evap = evap_rate * jax.nn.sigmoid(new[3])
        new[3] = new[3] - latent_heat * (evap * load)
        new[4] = new[4] / (1.0 + scavenge * load)
        for f in range(NF):
            fields[f, x] = new[f]
        moved[x] = held
        scale[x] = kept * (1.0 - evap)
        gain[x] = (spray_0[x] * kept + sprays) * (1.0 - evap)

def last(got_x, got_y, own_low, own_high, count, got_a, got_b, loads, spray_0, spray_1, nxt, nxt_nu, keep):
    block = count.shape
    operands = on_chip(got_x, got_y, own_low, own_high, count, got_a, got_b, loads, spray_0, spray_1, nxt, nxt_nu, keep)
    return pl.pallas_call(
        last_kernel,
        out_shape=(
            pltpu.VMEM((NF,) + block, F32),
            pltpu.VMEM(block, F32),
            pltpu.VMEM(block, F32),
            pltpu.VMEM(block, jnp.int32),
            pltpu.VMEM(nxt.shape, F32),
            pltpu.VMEM(nxt_nu.shape, F32),
            pltpu.VMEM(keep.shape, F32),
        ),
        in_specs=[VMEM] * 13,
        out_specs=(VMEM,) * 7,
        input_output_aliases={10: 4, 11: 5, 12: 6},
        scratch_shapes=[pltpu.VMEM((2, NF, block[0] + 16, block[2]), F32)] + [pltpu.VMEM(got_x.shape, F32)] * 2,
        compiler_params=LIMIT,
        cost_estimate=cost(LAST_COST),
        name="last_substep",
    )(*operands)[:4]


def droplets_kernel(fields, mass, above, scale, gain, moved, wind_out, heat_out, soot_out, mass_out, masses, sems):
    slots, depth = mass.shape[:2]
    pending = copies([(fields.at[0:3], wind_out), (fields.at[3], heat_out), (fields.at[4], soot_out)], sems)
    for x in range(depth):
        held, by, plus = moved[x], scale[x], gain[x]
        for k in range(slots):
            before = above[k, x] if x < 2 else mass[k, x - 2]
            masses[k, x] = jnp.where(held > k, before * by + plus, before)
        copy = pltpu.make_async_copy(masses.at[:, x], mass_out.at[:, x], sems.at[3 + x])
        copy.start()
        pending.append(copy)
    for copy in pending:
        copy.wait()


def droplets(fields, mass, above, scale, gain, moved):
    block = moved.shape
    return pl.pallas_call(
        droplets_kernel,
        out_shape=(
            jax.ShapeDtypeStruct((3,) + block, F32),
            jax.ShapeDtypeStruct(block, F32),
            jax.ShapeDtypeStruct(block, F32),
            jax.ShapeDtypeStruct(mass.shape, F32),
        ),
        in_specs=[VMEM] * 6,
        out_specs=(ANY,) * 4,
        scratch_shapes=[pltpu.VMEM(mass.shape, F32), pltpu.SemaphoreType.DMA((3 + block[0],))],
        compiler_params=LIMIT,
        name="droplets",
    )(*on_chip(fields, mass, above, scale, gain, moved))


def local(wind, heat, soot, mass, count, label, onset):
    chain, width = lax.axis_size("tun"), lax.axis_size("sec")
    pairs_a = [(i, i ^ 1) for i in range(chain)]
    pairs_b = [(i, ((i + 1) ^ 1) - 1) for i in range(1, chain - 1)]
    msg_b, msg_a, wind, heat, soot, mass, count, begins = pack_tun(onset, wind, heat, soot, mass, count, label)
    got_b = lax.ppermute(msg_b, "tun", pairs_b)
    got_a = lax.ppermute(msg_a, "tun", pairs_a)
    msg_x, msg_y, own_low, own_high = pack_sec(wind, heat, soot, mass, count, begins, got_a, got_b)
    got_x = lax.ppermute(msg_x, "sec", [(i, i ^ 1) for i in range(width)])
    got_y = lax.ppermute(msg_y, "sec", [(i, ((i + 1) ^ 1) - 1) for i in range(1, width - 1)])
    above = lax.ppermute(pack_mass(mass, begins), "tun", [(i, i + 1) for i in range(chain - 1)])
    count_out, nxt, nxt_nu, keep, loads, spray_0, spray_1 = first(
        wind, heat, soot, mass, count, begins, got_a, got_b, msg_x
    )
    fields, scale, gain, moved = last(
        got_x, got_y, own_low, own_high, count, got_a, got_b, loads, spray_0, spray_1, nxt, nxt_nu, keep
    )
    wind_out, heat_out, soot_out, mass_out = droplets(fields, mass, above, scale, gain, moved)
    return wind_out, heat_out, soot_out, mass_out, count_out


def solution(mesh):
    return jax.shard_map(
        local,
        mesh=mesh,
        in_specs=(
            P(None, "tun", "sec", None),
            P("tun", "sec", None),
            P("tun", "sec", None),
            P(None, "tun", "sec", None),
            P("tun", "sec", None),
            P("tun", "sec", None),
            P(),
        ),
        out_specs=(
            P(None, "tun", "sec", None),
            P("tun", "sec", None),
            P("tun", "sec", None),
            P(None, "tun", "sec", None),
            P("tun", "sec", None),
        ),
        check_vma=False,
    )
```

```python
import jax
import jax.numpy as jnp
from jax import lax
from jax.experimental import pallas as pl
from jax.experimental.pallas import tpu as pltpu
from jax.sharding import PartitionSpec as P

visc_base = 0.2
time_step = 0.1
buoyancy = 0.5
drag_rate = 0.3
vent_speed = 1.0
inject_rate = 0.5
evap_rate = 0.4
latent_heat = 0.5
scavenge = 0.3

NF = 5
F32 = jnp.float32
VMEM = pl.BlockSpec(memory_space=pltpu.VMEM)
SMEM = pl.BlockSpec(memory_space=pltpu.SMEM)
HBM = pl.BlockSpec(memory_space=pltpu.HBM)
ANY = pl.BlockSpec(memory_space=pl.ANY)
ROW = 8


FIRST_COST, LAST_COST = 3, 0


def cost(units):
    return pl.CostEstimate(flops=int(units * 1e9), transcendentals=0, bytes_accessed=int(units * 1e6))


LIMIT = pltpu.CompilerParams(vmem_limit_bytes=12 << 20)


def on_chip(*arrays):
    return tuple(pltpu.with_memory_space_constraint(a, pltpu.VMEM) for a in arrays)


def copies(pairs, sems):
    started = []
    for n, (src, dst) in enumerate(pairs):
        copy = pltpu.make_async_copy(src, dst, sems.at[n])
        copy.start()
        started.append(copy)
    return started

def live_sum(mass, count):
    total = jnp.zeros(count.shape, F32)
    for k in range(len(mass)):
        total = total + jnp.where(count > k, mass[k], 0.0)
    return total


def onset_of(label, onset):
    first = jnp.full(label.shape, 1 << 20, jnp.int32)
    for z in range(onset.shape[0]):
        first = jnp.where(label == z + 1, onset[z], first)
    return first


def pack_tun_kernel(
    onset, wind, heat, soot, mass, count, label,
    msg_b, msg_a, winds, heats, soots, tops, counts, begins, labels, onsets, sems,
):
    depth = heat.shape[0]
    odd = lax.axis_index("tun") % 2 == 1
    top = depth - 2
    start_a = jnp.where(odd, 0, top)
    start_b = top - start_a
    onset_copy, label_copy, count_copy, *others = copies(
        [
            (onset, onsets), (label, labels), (count, counts), (mass.at[:, top:depth], tops), (wind, winds), (heat, heats), (soot, soots)
        ],
        sems,
    )
    onset_copy.wait()
    label_copy.wait()
    for x in range(depth):
        begins[x] = onset_of(labels[x], onsets)
    count_copy.wait()
    others[0].wait()
    held = counts[top:depth]
    total = live_sum([tops[k] for k in range(tops.shape[0])], held)
    for copy in others[1:]:
        copy.wait()
    for start, msg in ((start_b, msg_b), (start_a, msg_a)):
        here = pl.ds(start, 2)
        for f in range(3):
            msg[f] = winds[f, here]
        msg[3] = heats[here]
        msg[4] = soots[here]
        msg[NF] = begins[here].astype(F32)
        msg[NF + 1] = held.astype(F32)
        msg[NF + 2] = total


def in_hbm(*arrays):
    return tuple(pltpu.with_memory_space_constraint(a, pltpu.HBM) for a in arrays)


def pack_tun(onset, wind, heat, soot, mass, count, label):
    arrays = (wind, heat, soot, mass, count, label)
    msg = pltpu.VMEM((NF + 3, 2) + heat.shape[1:], F32)
    return pl.pallas_call(
        pack_tun_kernel,
        out_shape=(msg, msg)
        + tuple(pltpu.VMEM(a.shape, a.dtype) for a in arrays[:3])
        + (pltpu.VMEM((mass.shape[0], 2) + mass.shape[2:], F32),)
        + tuple(pltpu.VMEM(a.shape, a.dtype) for a in arrays[4:]),
        in_specs=[HBM] * 7,
        out_specs=(VMEM,) * 8,
        scratch_shapes=[
            pltpu.VMEM(label.shape, jnp.int32),
            pltpu.SMEM(onset.shape, jnp.int32),
            pltpu.SemaphoreType.DMA((7,)),
        ],
        compiler_params=LIMIT,
        name="pack_tun",
    )(*in_hbm(onset, *arrays))


def pack_mass_kernel(tops, after, msg):
    msg[...] = tops[...]


def pack_mass(mass, after):
    return pl.pallas_call(
        pack_mass_kernel,
        out_shape=pltpu.VMEM(mass.shape, F32),
        in_specs=[VMEM] * 2,
        out_specs=VMEM,
        compiler_params=LIMIT,
        name="pack_mass",
    )(*on_chip(mass, after))


def pack_sec_kernel(got_b, got_a, wind, heat, soot, mass, count, begins, msg_x, msg_y, own_low, own_high, to_low, to_high):
    depth, rows, lanes = heat.shape
    slots = mass.shape[0]
    odd = lax.axis_index("tun") % 2 == 1

    def flat(ref):
        return ref.reshape(-1, lanes)

    winds, heats, soots, massed = flat(wind), flat(heat), flat(soot), flat(mass)
    counted, begun, from_a, from_b = flat(count), flat(begins), flat(got_a), flat(got_b)

    def own(f, row):
        ref, base = ((winds, f * depth * rows), (heats, 0), (soots, 0))[max(f - 2, 0)]
        return ref[pl.ds(base + row, depth, stride=rows), :]

    def beside(f, row):
        here = pl.ds(f * 2 * rows + row, 2, stride=rows)
        a, b = from_a[here, :], from_b[here, :]
        return jnp.where(odd, a, b), jnp.where(odd, b, a)

    for msg, kept, first, second in ((to_low, own_low, 0, 1), (to_high, own_high, rows - 1, rows - 2)):
        for f in range(NF):
            for n, row in ((f, first), (NF + f, second)):
                before, after = beside(f, row)
                centre = own(f, row)
                kept[n] = jnp.concatenate([before, centre, after], axis=0)
                msg[n] = centre
                if n < NF:
                    corner, place = 2 * NF + 1 + n // 4, 2 * (n % 4)
                    msg[corner, place : place + 2, :] = jnp.concatenate([before[1:], after[:1]], axis=0)
        here = pl.ds(first, depth, stride=rows)
        held = counted[here, :]
        sums = live_sum([massed[pl.ds(k * depth * rows + first, depth, stride=rows), :] for k in range(slots)], held)
        begins_up, begins_down = beside(NF, first)
        held_up, _ = beside(NF + 1, first)
        sums_up, _ = beside(NF + 2, first)
        starts = jnp.concatenate([begins_up[1:], begun[here, :].astype(F32), begins_down[:1]], axis=0)
        held = jnp.concatenate([held_up, held.astype(F32)], axis=0)
        sums = jnp.concatenate([sums_up, sums], axis=0)
        loads = sums + jnp.where(starts <= 0.0, inject_rate * held, 0.0)
        kept[2 * NF, 1 : 3 + depth, :] = loads
        msg[2 * NF] = loads[1 : 1 + depth]
    odd_row = lax.axis_index("sec") % 2 == 1
    for n in range(2 * NF + 3):
        lower, upper = to_low[n], to_high[n]
        msg_x[n] = jnp.where(odd_row, lower, upper)
        msg_y[n] = jnp.where(odd_row, upper, lower)


def pack_sec(wind, heat, soot, mass, count, begins, got_a, got_b):
    depth, rows, lanes = heat.shape
    msg = pltpu.VMEM((2 * NF + 3, depth, lanes), F32)
    kept = pltpu.VMEM((2 * NF + 1, depth + 4, lanes), F32)
    return pl.pallas_call(
        pack_sec_kernel,
        out_shape=(msg, msg, kept, kept),
        in_specs=[VMEM] * 8,
        out_specs=(VMEM,) * 4,
        scratch_shapes=[pltpu.VMEM((2 * NF + 3, depth, lanes), F32)] * 2,
        compiler_params=LIMIT,
        name="pack_sec",
    )(*on_chip(got_b, got_a, wind, heat, soot, mass, count, begins))


def viscosity(heat):
    return visc_base * (1.0 + 0.5 * jnp.tanh(heat))


def stencil(centre, nu, sides, nu_sides):
    lane = lax.broadcasted_iota(jnp.int32, nu.shape, 1)
    last = nu.shape[1] - 1
    rest = None
    weights = []
    for d in range(3):
        for side, sign in ((0, -1.0), (1, 1.0)):
            weight = (0.5 * time_step) * ((nu + nu_sides[d][side]) - sign * centre[d])
            rest = weight if rest is None else rest + weight
            if d == 2:
                weight = jnp.where(lane == (last if side else 0), 0.0, weight)
            weights.append(weight)
    rest = 1.0 - rest
    out = []
    for f in range(NF):
        value = rest * centre[f]
        for d in range(3):
            for side in (0, 1):
                value = value + weights[2 * d + side] * sides[d][side](f)
        out.append(value)
    out[0] = out[0] + (time_step * drag_rate) * (vent_speed - centre[0])
    out[2] = out[2] + (time_step * buoyancy) * centre[3]
    return out


def around(plane):
    return pltpu.roll(plane, 1, 1), pltpu.roll(plane, plane.shape[1] - 1, 1)


def nu_around(nu):
    lane = lax.broadcasted_iota(jnp.int32, nu.shape, 1)
    low, high = around(nu)
    return jnp.where(lane == 0, visc_base, low), jnp.where(lane == nu.shape[1] - 1, visc_base, high)


def first_kernel(
    wind, heat, soot, mass, count, begins, got_a, got_b, after,
    count_out, nxt, nxt_nu, keep, loads, spray_0, spray_1,
    ext, ext_nu, counts, sems,
):
    depth, rows, lanes = heat.shape
    slots = mass.shape[0]
    tall = rows + 2 * ROW
    tun = lax.axis_index("tun")
    odd = tun % 2 == 1
    own = [wind.at[0], wind.at[1], wind.at[2], heat, soot]

    def beside(n, x):
        return jnp.where(odd, got_a[n, x], got_b[n, x]), jnp.where(odd, got_b[n, x], got_a[n, x])

    def put(ref, plane, value):
        ref[plane * tall + ROW : plane * tall + ROW + rows, :] = value

    def at(ref, plane, shift=0):
        return ref[plane * tall + ROW + shift : plane * tall + ROW + shift + rows, :]

    planes = depth + 4
    for f in range(NF):
        for x in range(depth):
            put(ext, f * planes + x + 2, own[f][x])
        for x in (0, 1):
            before, behind = beside(f, x)
            put(ext, f * planes + x, before)
            put(ext, f * planes + depth + 2 + x, behind)
    for x in range(planes):
        put(ext_nu, x, viscosity(at(ext, 3 * planes + x)))

    for x in (0, 1):
        counts[x] = beside(NF + 1, x)[0].astype(jnp.int32)
    for x in range(depth - 2):
        counts[x + 2] = count[x]
    pending = copies([(counts, count_out)], sems)

    for x in range(-1, depth + 1):
        centre = [at(ext, f * planes + x + 2) for f in range(NF)]
        nu = at(ext_nu, x + 2)
        lifted = [around(c) for c in centre]
        sides = [
            (lambda f: at(ext, f * planes + x + 1), lambda f: at(ext, f * planes + x + 3)),
            (lambda f: at(ext, f * planes + x + 2, -1), lambda f: at(ext, f * planes + x + 2, 1)),
            (lambda f: lifted[f][0], lambda f: lifted[f][1]),
        ]
        nu_sides = [
            (at(ext_nu, x + 1), at(ext_nu, x + 3)),
            (at(ext_nu, x + 2, -1), at(ext_nu, x + 2, 1)),
            nu_around(nu),
        ]
        new = stencil(centre, nu, sides, nu_sides)
        if x < 1:
            moved_total, moved_count = beside(NF + 2, x + 1)[0], beside(NF + 1, x + 1)[0]
        else:
            held = count[x - 1]
            moved_total, moved_count = live_sum([mass[k, x - 1] for k in range(slots)], held), held.astype(F32)
        if x < 0:
            start = beside(NF, 1)[0].astype(jnp.int32)
        elif x < depth:
            start = begins[x]
        else:
            start = beside(NF, 0)[1].astype(jnp.int32)
        sprays = jnp.where(start <= 0, inject_rate, 0.0)
        load = moved_total + sprays * moved_count
        evap = evap_rate * jax.nn.sigmoid(new[3])
        new[3] = new[3] - latent_heat * (evap * load)
        new[4] = new[4] / (1.0 + scavenge * load)
        if x < depth:
            keep[(x + 1) * rows : (x + 2) * rows, :] = 1.0 - evap
            loads[x + 1] = load
            spray_0[x + 1] = sprays
        if 0 <= x < depth:
            spray_1[x] = jnp.where(start <= 1, inject_rate, 0.0)
        inside = tun > 0 if x < 0 else tun < lax.axis_size("tun") - 1 if x == depth else None
        for f in range(NF):
            value = new[f] if inside is None else jnp.where(inside, new[f], 0.0)
            put(nxt, f * (depth + 2) + x + 1, value)
            if f == 3:
                put(nxt_nu, x + 1, viscosity(value))
    for copy in pending:
        copy.wait()


def first(wind, heat, soot, mass, count, begins, got_a, got_b, after):
    depth, rows, lanes = heat.shape
    tall = rows + 2 * ROW
    return pl.pallas_call(
        first_kernel,
        out_shape=(
            jax.ShapeDtypeStruct(count.shape, jnp.int32),
            pltpu.VMEM((NF * (depth + 2) * tall, lanes), F32),
            pltpu.VMEM(((depth + 2) * tall, lanes), F32),
            pltpu.VMEM(((depth + 1) * rows, lanes), F32),
            pltpu.VMEM((depth + 1, rows, lanes), F32),
            pltpu.VMEM((depth + 1, rows, lanes), F32),
            pltpu.VMEM((depth, rows, lanes), F32),
        ),
        in_specs=[VMEM] * 8 + [ANY],
        out_specs=(ANY,) + (VMEM,) * 6,
        scratch_shapes=[
            pltpu.VMEM((NF * (depth + 4) * tall, lanes), F32),
            pltpu.VMEM(((depth + 4) * tall, lanes), F32),
            pltpu.VMEM((depth, rows, lanes), jnp.int32),
            pltpu.SemaphoreType.DMA((1,)),
        ],
        compiler_params=LIMIT,
        cost_estimate=cost(FIRST_COST),
        name="first_substep",
    )(*on_chip(wind, heat, soot, mass, count, begins, got_a, got_b), after)


def last_kernel(
    got_x, got_y, above, own_low, own_high, mass, count, got_a, got_b, loads, spray_0, spray_1, nxt_in, nxt_nu_in, keep_in,
    wind_out, heat_out, soot_out, mass_out, nxt, nxt_nu, keep,
    beside, low, high, fields, masses, sems,
):
    slots, depth, rows, lanes = mass.shape
    tall = rows + 2 * ROW
    planes = depth + 2
    tun, sec = lax.axis_index("tun"), lax.axis_index("sec")
    odd = tun % 2 == 1
    inside_up, inside_down = tun > 0, tun < lax.axis_size("tun") - 1
    odd_row = sec % 2 == 1
    for n in range(2 * NF + 3):
        x, y = got_x[n], got_y[n]
        low[n] = jnp.where(odd_row, x, y)
        high[n] = jnp.where(odd_row, y, x)

    place = lax.broadcasted_iota(jnp.int32, (planes, lanes), 0)
    inside = ((place > 0) | inside_up) & ((place < planes - 1) | inside_down)

    def step(centre, nu, sides, nu_sides, load):
        new = stencil(centre, nu, sides, nu_sides)
        evap = evap_rate * jax.nn.sigmoid(new[3])
        new[3] = new[3] - latent_heat * (evap * load)
        new[4] = new[4] / (1.0 + scavenge * load)
        return new, 1.0 - evap

    for flip, (got, own, outer_row, inner_row, there) in enumerate(
        (
            (low, own_low, ROW - 1, 0, sec > 0),
            (high, own_high, ROW + rows, rows - 1, sec < lax.axis_size("sec") - 1),
        )
    ):
        line = beside.at[flip]
        for f in range(NF):
            corner, spot = 2 * NF + 1 + f // 4, 2 * (f % 4)
            line[f, 8 : 8 + depth, :] = got[f]
            line[f, 7:8, :] = got[corner, spot : spot + 1, :]
            line[f, 8 + depth : 9 + depth, :] = got[corner, spot + 1 : spot + 2, :]
        wide, block = slice(7, 9 + depth), slice(8, 8 + depth)
        line_nu, own_nu = viscosity(line[3, wide, :]), viscosity(own[3])

        def ordered(near, far, swap):
            return (near, far) if swap else (far, near)

        centre = [line[f, block, :] for f in range(NF)]
        lifted = [around(c) for c in centre]
        nu = line_nu[1 : 1 + depth]
        new, _ = step(
            centre,
            nu,
            [
                (lambda f: line[f, 7 : 7 + depth, :], lambda f: line[f, 9 : 9 + depth, :]),
                ordered(lambda f: own[f, 2 : 2 + depth, :], lambda f: got[NF + f], flip == 1),
                (lambda f: lifted[f][0], lambda f: lifted[f][1]),
            ],
            [
                (line_nu[0:depth], line_nu[2 : 2 + depth]),
                ordered(own_nu[2 : 2 + depth], viscosity(got[NF + 3]), flip == 1),
                nu_around(nu),
            ],
            got[2 * NF],
        )
        for f in range(NF):
            value = jnp.where(there, new[f], 0.0)
            nxt[pl.ds((f * planes + 1) * tall + outer_row, depth, stride=tall), :] = value
            if f == 3:
                nxt_nu[pl.ds(tall + outer_row, depth, stride=tall), :] = viscosity(value)

        mid = slice(1, 1 + planes)
        centre = [own[f, mid, :] for f in range(NF)]
        lifted = [around(c) for c in centre]
        nu = own_nu[mid]
        new, left = step(
            centre,
            nu,
            [
                (lambda f: own[f, 0:planes, :], lambda f: own[f, 2 : 2 + planes, :]),
                ordered(lambda f: line[f, wide, :], lambda f: own[NF + f, mid, :], flip == 0),
                (lambda f: lifted[f][0], lambda f: lifted[f][1]),
            ],
            [
                (own_nu[0:planes], own_nu[2 : 2 + planes]),
                ordered(line_nu, viscosity(own[NF + 3, mid, :]), flip == 0),
                nu_around(nu),
            ],
            own[2 * NF, mid, :],
        )
        for f in range(NF):
            value = jnp.where(inside, new[f], 0.0)
            nxt[pl.ds(f * planes * tall + ROW + inner_row, planes, stride=tall), :] = value
            if f == 3:
                nxt_nu[pl.ds(ROW + inner_row, planes, stride=tall), :] = viscosity(value)
        keep[pl.ds(inner_row, depth + 1, stride=rows), :] = left[: depth + 1]

    def at(ref, plane, shift=0):
        return ref[plane * tall + ROW + shift : plane * tall + ROW + shift + rows, :]

    pending = []
    half = depth // 2
    for x in range(depth):
        centre = [at(nxt, f * planes + x + 1) for f in range(NF)]
        nu = at(nxt_nu, x + 1)
        lifted = [around(c) for c in centre]
        sides = [
            (lambda f: at(nxt, f * planes + x), lambda f: at(nxt, f * planes + x + 2)),
            (lambda f: at(nxt, f * planes + x + 1, -1), lambda f: at(nxt, f * planes + x + 1, 1)),
            (lambda f: lifted[f][0], lambda f: lifted[f][1]),
        ]
        nu_sides = [
            (at(nxt_nu, x), at(nxt_nu, x + 2)),
            (at(nxt_nu, x + 1, -1), at(nxt_nu, x + 1, 1)),
            nu_around(nu),
        ]
        new = stencil(centre, nu, sides, nu_sides)
        if x < 2:
            held = jnp.where(odd, got_a[NF + 1, x], got_b[NF + 1, x]).astype(jnp.int32)
        else:
            held = count[x - 2]
        kept = keep[x * rows : (x + 1) * rows, :]
        sprays = spray_1[x]
        load = loads[x] * kept + sprays * held.astype(F32)
        evap = evap_rate * jax.nn.sigmoid(new[3])
        new[3] = new[3] - latent_heat * (evap * load)
        new[4] = new[4] / (1.0 + scavenge * load)
        for f in range(NF):
            fields[f, x] = new[f]
        by = kept * (1.0 - evap)
        plus = (spray_0[x] * kept + sprays) * (1.0 - evap)
        for k in range(slots):
            before = above[k, x] if x < 2 else mass[k, x - 2]
            masses[k, x] = jnp.where(held > k, before * by + plus, before)
        copy = pltpu.make_async_copy(masses.at[:, x], mass_out.at[:, x], sems.at[x])
        copy.start()
        pending.append(copy)
        if x % half == half - 1:
            done = slice(x + 1 - half, x + 1)
            pending += copies(
                [
                    (fields.at[0:3, done], wind_out.at[:, done]),
                    (fields.at[3, done], heat_out.at[done]),
                    (fields.at[4, done], soot_out.at[done]),
                ],
                sems.at[depth + 3 * (x // half) : depth + 3 * (x // half) + 3],
            )
    for copy in pending:
        copy.wait()

def last(got_x, got_y, above, own_low, own_high, mass, count, got_a, got_b, loads, spray_0, spray_1, nxt, nxt_nu, keep):
    block = count.shape
    operands = on_chip(got_x, got_y, above, own_low, own_high, mass, count, got_a, got_b, loads, spray_0, spray_1, nxt, nxt_nu, keep)
    return pl.pallas_call(
        last_kernel,
        out_shape=(
            jax.ShapeDtypeStruct((3,) + block, F32),
            jax.ShapeDtypeStruct(block, F32),
            jax.ShapeDtypeStruct(block, F32),
            jax.ShapeDtypeStruct(mass.shape, F32),
            pltpu.VMEM(nxt.shape, F32),
            pltpu.VMEM(nxt_nu.shape, F32),
            pltpu.VMEM(keep.shape, F32),
        ),
        in_specs=[VMEM] * 15,
        out_specs=(ANY,) * 4 + (VMEM,) * 3,
        input_output_aliases={12: 4, 13: 5, 14: 6},
        scratch_shapes=[
            pltpu.VMEM((2, NF, block[0] + 16, block[2]), F32),
            pltpu.VMEM(got_x.shape, F32),
            pltpu.VMEM(got_x.shape, F32),
            pltpu.VMEM((NF,) + block, F32),
            pltpu.VMEM(mass.shape, F32),
            pltpu.SemaphoreType.DMA((6 + block[0],)),
        ],
        compiler_params=LIMIT,
        cost_estimate=cost(LAST_COST),
        name="last_substep",
    )(*operands)[:4]


def local(wind, heat, soot, mass, count, label, onset):
    chain, width = lax.axis_size("tun"), lax.axis_size("sec")
    pairs_a = [(i, i ^ 1) for i in range(chain)]
    pairs_b = [(i, ((i + 1) ^ 1) - 1) for i in range(1, chain - 1)]
    msg_b, msg_a, wind, heat, soot, tops, count, begins = pack_tun(onset, wind, heat, soot, mass, count, label)
    got_b = lax.ppermute(msg_b, "tun", pairs_b)
    got_a = lax.ppermute(msg_a, "tun", pairs_a)
    msg_x, msg_y, own_low, own_high = pack_sec(wind, heat, soot, mass, count, begins, got_a, got_b)
    got_x = lax.ppermute(msg_x, "sec", [(i, i ^ 1) for i in range(width)])
    got_y = lax.ppermute(msg_y, "sec", [(i, ((i + 1) ^ 1) - 1) for i in range(1, width - 1)])
    above = lax.ppermute(pack_mass(tops, begins), "tun", [(i, i + 1) for i in range(chain - 1)])
    count_out, nxt, nxt_nu, keep, loads, spray_0, spray_1 = first(
        wind, heat, soot, mass, count, begins, got_a, got_b, own_low
    )
    wind_out, heat_out, soot_out, mass_out = last(
        got_x, got_y, above, own_low, own_high, mass, count, got_a, got_b, loads, spray_0, spray_1, nxt, nxt_nu, keep
    )
    return wind_out, heat_out, soot_out, mass_out, count_out


def solution(mesh):
    return jax.shard_map(
        local,
        mesh=mesh,
        in_specs=(
            P(None, "tun", "sec", None),
            P("tun", "sec", None),
            P("tun", "sec", None),
            P(None, "tun", "sec", None),
            P("tun", "sec", None),
            P("tun", "sec", None),
            P(),
        ),
        out_specs=(
            P(None, "tun", "sec", None),
            P("tun", "sec", None),
            P("tun", "sec", None),
            P(None, "tun", "sec", None),
            P("tun", "sec", None),
        ),
        check_vma=False,
    )
```

```python
import jax
import jax.numpy as jnp
from jax import lax
from jax.experimental import pallas as pl
from jax.experimental.pallas import tpu as pltpu
from jax.sharding import PartitionSpec as P

visc_base = 0.2
time_step = 0.1
buoyancy = 0.5
drag_rate = 0.3
vent_speed = 1.0
inject_rate = 0.5
evap_rate = 0.4
latent_heat = 0.5
scavenge = 0.3

NF = 5
F32 = jnp.float32
VMEM = pl.BlockSpec(memory_space=pltpu.VMEM)
SMEM = pl.BlockSpec(memory_space=pltpu.SMEM)
HBM = pl.BlockSpec(memory_space=pltpu.HBM)
ANY = pl.BlockSpec(memory_space=pl.ANY)
ROW = 8


FIRST_COST, LAST_COST = 3, 0


def cost(units):
    return pl.CostEstimate(flops=int(units * 1e9), transcendentals=0, bytes_accessed=int(units * 1e6))


LIMIT = pltpu.CompilerParams(vmem_limit_bytes=12 << 20)


def on_chip(*arrays):
    return tuple(pltpu.with_memory_space_constraint(a, pltpu.VMEM) for a in arrays)


def copies(pairs, sems):
    started = []
    for n, (src, dst) in enumerate(pairs):
        copy = pltpu.make_async_copy(src, dst, sems.at[n])
        copy.start()
        started.append(copy)
    return started

def live_sum(mass, count):
    total = jnp.zeros(count.shape, F32)
    for k in range(len(mass)):
        total = total + jnp.where(count > k, mass[k], 0.0)
    return total


def onset_of(label, onset):
    first = jnp.full(label.shape, 1 << 20, jnp.int32)
    for z in range(onset.shape[0]):
        first = jnp.where(label == z + 1, onset[z], first)
    return first


def pack_tun_kernel(
    onset, wind, heat, soot, mass, count, label,
    msg_b, msg_a, tops, begins, held_ref, labels, onsets, sems,
):
    depth = heat.shape[0]
    odd = lax.axis_index("tun") % 2 == 1
    top = depth - 2
    start_a = jnp.where(odd, 0, top)
    start_b = top - start_a
    pairs = [
        (onset, onsets), (label, labels), (count.at[top:depth], held_ref), (mass.at[:, top:depth], tops)
    ]
    for start, msg in ((start_b, msg_b), (start_a, msg_a)):
        here = pl.ds(start, 2)
        pairs += [(wind.at[:, here], msg.at[0:3]), (heat.at[here], msg.at[3]), (soot.at[here], msg.at[4])]
    onset_copy, label_copy, count_copy, *others = copies(pairs, sems)
    onset_copy.wait()
    label_copy.wait()
    for x in range(depth):
        begins[x] = onset_of(labels[x], onsets)
    count_copy.wait()
    held = held_ref[...]
    others[0].wait()
    total = live_sum([tops[k] for k in range(tops.shape[0])], held)
    for copy in others[1:]:
        copy.wait()
    for start, msg in ((start_b, msg_b), (start_a, msg_a)):
        msg[NF] = begins[pl.ds(start, 2)].astype(F32)
        msg[NF + 1] = held.astype(F32)
        msg[NF + 2] = total


def in_hbm(*arrays):
    return tuple(pltpu.with_memory_space_constraint(a, pltpu.HBM) for a in arrays)


def pack_tun(onset, wind, heat, soot, mass, count, label):
    arrays = (wind, heat, soot, mass, count, label)
    msg = pltpu.VMEM((NF + 3, 2) + heat.shape[1:], F32)
    return pl.pallas_call(
        pack_tun_kernel,
        out_shape=(
            msg,
            msg,
            pltpu.VMEM((mass.shape[0], 2) + mass.shape[2:], F32),
            pltpu.VMEM(label.shape, jnp.int32),
        ),
        in_specs=[HBM] * 7,
        out_specs=(VMEM,) * 4,
        scratch_shapes=[
            pltpu.VMEM((2,) + label.shape[1:], jnp.int32),
            pltpu.VMEM(label.shape, jnp.int32),
            pltpu.SMEM(onset.shape, jnp.int32),
            pltpu.SemaphoreType.DMA((10,)),
        ],
        compiler_params=LIMIT,
        name="pack_tun",
    )(*in_hbm(onset, *arrays))


def pack_mass_kernel(tops, after, msg):
    msg[...] = tops[...]


def pack_mass(mass, after):
    return pl.pallas_call(
        pack_mass_kernel,
        out_shape=pltpu.VMEM(mass.shape, F32),
        in_specs=[VMEM] * 2,
        out_specs=VMEM,
        compiler_params=LIMIT,
        name="pack_mass",
    )(*on_chip(mass, after))


def pack_sec_kernel(got_b, got_a, wind, heat, soot, mass, count, begins, msg_x, msg_y, own_low, own_high, to_low, to_high):
    depth, rows, lanes = heat.shape
    slots = mass.shape[0]
    odd = lax.axis_index("tun") % 2 == 1

    def flat(ref):
        return ref.reshape(-1, lanes)

    winds, heats, soots, massed = flat(wind), flat(heat), flat(soot), flat(mass)
    counted, begun, from_a, from_b = flat(count), flat(begins), flat(got_a), flat(got_b)

    def own(f, row):
        ref, base = ((winds, f * depth * rows), (heats, 0), (soots, 0))[max(f - 2, 0)]
        return ref[pl.ds(base + row, depth, stride=rows), :]

    def beside(f, row):
        here = pl.ds(f * 2 * rows + row, 2, stride=rows)
        a, b = from_a[here, :], from_b[here, :]
        return jnp.where(odd, a, b), jnp.where(odd, b, a)

    for msg, kept, first, second in ((to_low, own_low, 0, 1), (to_high, own_high, rows - 1, rows - 2)):
        for f in range(NF):
            for n, row in ((f, first), (NF + f, second)):
                before, after = beside(f, row)
                centre = own(f, row)
                kept[n] = jnp.concatenate([before, centre, after], axis=0)
                msg[n] = centre
                if n < NF:
                    corner, place = 2 * NF + 1 + n // 4, 2 * (n % 4)
                    msg[corner, place : place + 2, :] = jnp.concatenate([before[1:], after[:1]], axis=0)
        here = pl.ds(first, depth, stride=rows)
        held = counted[here, :]
        sums = live_sum([massed[pl.ds(k * depth * rows + first, depth, stride=rows), :] for k in range(slots)], held)
        begins_up, begins_down = beside(NF, first)
        held_up, _ = beside(NF + 1, first)
        sums_up, _ = beside(NF + 2, first)
        starts = jnp.concatenate([begins_up[1:], begun[here, :].astype(F32), begins_down[:1]], axis=0)
        held = jnp.concatenate([held_up, held.astype(F32)], axis=0)
        sums = jnp.concatenate([sums_up, sums], axis=0)
        loads = sums + jnp.where(starts <= 0.0, inject_rate * held, 0.0)
        kept[2 * NF, 1 : 3 + depth, :] = loads
        msg[2 * NF] = loads[1 : 1 + depth]
    odd_row = lax.axis_index("sec") % 2 == 1
    for n in range(2 * NF + 3):
        lower, upper = to_low[n], to_high[n]
        msg_x[n] = jnp.where(odd_row, lower, upper)
        msg_y[n] = jnp.where(odd_row, upper, lower)


def pack_sec(wind, heat, soot, mass, count, begins, got_a, got_b):
    depth, rows, lanes = heat.shape
    msg = pltpu.VMEM((2 * NF + 3, depth, lanes), F32)
    kept = pltpu.VMEM((2 * NF + 1, depth + 4, lanes), F32)
    return pl.pallas_call(
        pack_sec_kernel,
        out_shape=(msg, msg, kept, kept),
        in_specs=[VMEM] * 8,
        out_specs=(VMEM,) * 4,
        scratch_shapes=[pltpu.VMEM((2 * NF + 3, depth, lanes), F32)] * 2,
        compiler_params=LIMIT,
        name="pack_sec",
    )(*on_chip(got_b, got_a, wind, heat, soot, mass, count, begins))


def viscosity(heat):
    return visc_base * (1.0 + 0.5 * jnp.tanh(heat))


def stencil(centre, nu, sides, nu_sides):
    lane = lax.broadcasted_iota(jnp.int32, nu.shape, 1)
    last = nu.shape[1] - 1
    rest = None
    weights = []
    for d in range(3):
        for side, sign in ((0, -1.0), (1, 1.0)):
            weight = (0.5 * time_step) * ((nu + nu_sides[d][side]) - sign * centre[d])
            rest = weight if rest is None else rest + weight
            if d == 2:
                weight = jnp.where(lane == (last if side else 0), 0.0, weight)
            weights.append(weight)
    rest = 1.0 - rest
    out = []
    for f in range(NF):
        value = rest * centre[f]
        for d in range(3):
            for side in (0, 1):
                value = value + weights[2 * d + side] * sides[d][side](f)
        out.append(value)
    out[0] = out[0] + (time_step * drag_rate) * (vent_speed - centre[0])
    out[2] = out[2] + (time_step * buoyancy) * centre[3]
    return out


def around(plane):
    return pltpu.roll(plane, 1, 1), pltpu.roll(plane, plane.shape[1] - 1, 1)


def nu_around(nu):
    lane = lax.broadcasted_iota(jnp.int32, nu.shape, 1)
    low, high = around(nu)
    return jnp.where(lane == 0, visc_base, low), jnp.where(lane == nu.shape[1] - 1, visc_base, high)


def first_kernel(
    wind, heat, soot, mass, count, begins, got_a, got_b, after,
    count_out, nxt, nxt_nu, keep, loads, spray_0, spray_1,
    ext, ext_nu, counts, sems,
):
    depth, rows, lanes = heat.shape
    slots = mass.shape[0]
    tall = rows + 2 * ROW
    tun = lax.axis_index("tun")
    odd = tun % 2 == 1
    own = [wind.at[0], wind.at[1], wind.at[2], heat, soot]

    def beside(n, x):
        return jnp.where(odd, got_a[n, x], got_b[n, x]), jnp.where(odd, got_b[n, x], got_a[n, x])

    def put(ref, plane, value):
        ref[plane * tall + ROW : plane * tall + ROW + rows, :] = value

    def at(ref, plane, shift=0):
        return ref[plane * tall + ROW + shift : plane * tall + ROW + shift + rows, :]

    planes = depth + 4
    for f in range(NF):
        for x in range(depth):
            put(ext, f * planes + x + 2, own[f][x])
        for x in (0, 1):
            before, behind = beside(f, x)
            put(ext, f * planes + x, before)
            put(ext, f * planes + depth + 2 + x, behind)
    for x in range(planes):
        put(ext_nu, x, viscosity(at(ext, 3 * planes + x)))

    for x in (0, 1):
        counts[x] = beside(NF + 1, x)[0].astype(jnp.int32)
    for x in range(depth - 2):
        counts[x + 2] = count[x]
    pending = copies([(counts, count_out)], sems)

    for x in range(-1, depth + 1):
        centre = [at(ext, f * planes + x + 2) for f in range(NF)]
        nu = at(ext_nu, x + 2)
        lifted = [around(c) for c in centre]
        sides = [
            (lambda f: at(ext, f * planes + x + 1), lambda f: at(ext, f * planes + x + 3)),
            (lambda f: at(ext, f * planes + x + 2, -1), lambda f: at(ext, f * planes + x + 2, 1)),
            (lambda f: lifted[f][0], lambda f: lifted[f][1]),
        ]
        nu_sides = [
            (at(ext_nu, x + 1), at(ext_nu, x + 3)),
            (at(ext_nu, x + 2, -1), at(ext_nu, x + 2, 1)),
            nu_around(nu),
        ]
        new = stencil(centre, nu, sides, nu_sides)
        if x < 1:
            moved_total, moved_count = beside(NF + 2, x + 1)[0], beside(NF + 1, x + 1)[0]
        else:
            held = count[x - 1]
            moved_total, moved_count = live_sum([mass[k, x - 1] for k in range(slots)], held), held.astype(F32)
        if x < 0:
            start = beside(NF, 1)[0].astype(jnp.int32)
        elif x < depth:
            start = begins[x]
        else:
            start = beside(NF, 0)[1].astype(jnp.int32)
        sprays = jnp.where(start <= 0, inject_rate, 0.0)
        load = moved_total + sprays * moved_count
        evap = evap_rate * jax.nn.sigmoid(new[3])
        new[3] = new[3] - latent_heat * (evap * load)
        new[4] = new[4] / (1.0 + scavenge * load)
        if x < depth:
            keep[(x + 1) * rows : (x + 2) * rows, :] = 1.0 - evap
            loads[x + 1] = load
            spray_0[x + 1] = sprays
        if 0 <= x < depth:
            spray_1[x] = jnp.where(start <= 1, inject_rate, 0.0)
        inside = tun > 0 if x < 0 else tun < lax.axis_size("tun") - 1 if x == depth else None
        for f in range(NF):
            value = new[f] if inside is None else jnp.where(inside, new[f], 0.0)
            put(nxt, f * (depth + 2) + x + 1, value)
            if f == 3:
                put(nxt_nu, x + 1, viscosity(value))
    for copy in pending:
        copy.wait()


def first(wind, heat, soot, mass, count, begins, got_a, got_b, after):
    depth, rows, lanes = heat.shape
    tall = rows + 2 * ROW
    return pl.pallas_call(
        first_kernel,
        out_shape=(
            jax.ShapeDtypeStruct(count.shape, jnp.int32),
            pltpu.VMEM((NF * (depth + 2) * tall, lanes), F32),
            pltpu.VMEM(((depth + 2) * tall, lanes), F32),
            pltpu.VMEM(((depth + 1) * rows, lanes), F32),
            pltpu.VMEM((depth + 1, rows, lanes), F32),
            pltpu.VMEM((depth + 1, rows, lanes), F32),
            pltpu.VMEM((depth, rows, lanes), F32),
        ),
        in_specs=[VMEM] * 8 + [ANY],
        out_specs=(ANY,) + (VMEM,) * 6,
        scratch_shapes=[
            pltpu.VMEM((NF * (depth + 4) * tall, lanes), F32),
            pltpu.VMEM(((depth + 4) * tall, lanes), F32),
            pltpu.VMEM((depth, rows, lanes), jnp.int32),
            pltpu.SemaphoreType.DMA((1,)),
        ],
        compiler_params=LIMIT,
        cost_estimate=cost(FIRST_COST),
        name="first_substep",
    )(*on_chip(wind, heat, soot, mass, count, begins, got_a, got_b), after)


def last_kernel(
    got_x, got_y, above, own_low, own_high, mass, count, got_a, got_b, loads, spray_0, spray_1, nxt_in, nxt_nu_in, keep_in,
    wind_out, heat_out, soot_out, mass_out, nxt, nxt_nu, keep,
    beside, low, high, fields, masses, sems,
):
    slots, depth, rows, lanes = mass.shape
    tall = rows + 2 * ROW
    planes = depth + 2
    tun, sec = lax.axis_index("tun"), lax.axis_index("sec")
    odd = tun % 2 == 1
    inside_up, inside_down = tun > 0, tun < lax.axis_size("tun") - 1
    odd_row = sec % 2 == 1
    for n in range(2 * NF + 3):
        x, y = got_x[n], got_y[n]
        low[n] = jnp.where(odd_row, x, y)
        high[n] = jnp.where(odd_row, y, x)

    place = lax.broadcasted_iota(jnp.int32, (planes, lanes), 0)
    inside = ((place > 0) | inside_up) & ((place < planes - 1) | inside_down)

    def step(centre, nu, sides, nu_sides, load):
        new = stencil(centre, nu, sides, nu_sides)
        evap = evap_rate * jax.nn.sigmoid(new[3])
        new[3] = new[3] - latent_heat * (evap * load)
        new[4] = new[4] / (1.0 + scavenge * load)
        return new, 1.0 - evap

    for flip, (got, own, outer_row, inner_row, there) in enumerate(
        (
            (low, own_low, ROW - 1, 0, sec > 0),
            (high, own_high, ROW + rows, rows - 1, sec < lax.axis_size("sec") - 1),
        )
    ):
        line = beside.at[flip]
        for f in range(NF):
            corner, spot = 2 * NF + 1 + f // 4, 2 * (f % 4)
            line[f, 8 : 8 + depth, :] = got[f]
            line[f, 7:8, :] = got[corner, spot : spot + 1, :]
            line[f, 8 + depth : 9 + depth, :] = got[corner, spot + 1 : spot + 2, :]
        wide, block = slice(7, 9 + depth), slice(8, 8 + depth)
        line_nu, own_nu = viscosity(line[3, wide, :]), viscosity(own[3])

        def ordered(near, far, swap):
            return (near, far) if swap else (far, near)

        centre = [line[f, block, :] for f in range(NF)]
        lifted = [around(c) for c in centre]
        nu = line_nu[1 : 1 + depth]
        new, _ = step(
            centre,
            nu,
            [
                (lambda f: line[f, 7 : 7 + depth, :], lambda f: line[f, 9 : 9 + depth, :]),
                ordered(lambda f: own[f, 2 : 2 + depth, :], lambda f: got[NF + f], flip == 1),
                (lambda f: lifted[f][0], lambda f: lifted[f][1]),
            ],
            [
                (line_nu[0:depth], line_nu[2 : 2 + depth]),
                ordered(own_nu[2 : 2 + depth], viscosity(got[NF + 3]), flip == 1),
                nu_around(nu),
            ],
            got[2 * NF],
        )
        for f in range(NF):
            value = jnp.where(there, new[f], 0.0)
            nxt[pl.ds((f * planes + 1) * tall + outer_row, depth, stride=tall), :] = value
            if f == 3:
                nxt_nu[pl.ds(tall + outer_row, depth, stride=tall), :] = viscosity(value)

        mid = slice(1, 1 + planes)
        centre = [own[f, mid, :] for f in range(NF)]
        lifted = [around(c) for c in centre]
        nu = own_nu[mid]
        new, left = step(
            centre,
            nu,
            [
                (lambda f: own[f, 0:planes, :], lambda f: own[f, 2 : 2 + planes, :]),
                ordered(lambda f: line[f, wide, :], lambda f: own[NF + f, mid, :], flip == 0),
                (lambda f: lifted[f][0], lambda f: lifted[f][1]),
            ],
            [
                (own_nu[0:planes], own_nu[2 : 2 + planes]),
                ordered(line_nu, viscosity(own[NF + 3, mid, :]), flip == 0),
                nu_around(nu),
            ],
            own[2 * NF, mid, :],
        )
        for f in range(NF):
            value = jnp.where(inside, new[f], 0.0)
            nxt[pl.ds(f * planes * tall + ROW + inner_row, planes, stride=tall), :] = value
            if f == 3:
                nxt_nu[pl.ds(ROW + inner_row, planes, stride=tall), :] = viscosity(value)
        keep[pl.ds(inner_row, depth + 1, stride=rows), :] = left[: depth + 1]

    def at(ref, plane, shift=0):
        return ref[plane * tall + ROW + shift : plane * tall + ROW + shift + rows, :]

    pending = []
    half = depth // 2
    for x in range(depth):
        centre = [at(nxt, f * planes + x + 1) for f in range(NF)]
        nu = at(nxt_nu, x + 1)
        lifted = [around(c) for c in centre]
        sides = [
            (lambda f: at(nxt, f * planes + x), lambda f: at(nxt, f * planes + x + 2)),
            (lambda f: at(nxt, f * planes + x + 1, -1), lambda f: at(nxt, f * planes + x + 1, 1)),
            (lambda f: lifted[f][0], lambda f: lifted[f][1]),
        ]
        nu_sides = [
            (at(nxt_nu, x), at(nxt_nu, x + 2)),
            (at(nxt_nu, x + 1, -1), at(nxt_nu, x + 1, 1)),
            nu_around(nu),
        ]
        new = stencil(centre, nu, sides, nu_sides)
        if x < 2:
            held = jnp.where(odd, got_a[NF + 1, x], got_b[NF + 1, x]).astype(jnp.int32)
        else:
            held = count[x - 2]
        kept = keep[x * rows : (x + 1) * rows, :]
        sprays = spray_1[x]
        load = loads[x] * kept + sprays * held.astype(F32)
        evap = evap_rate * jax.nn.sigmoid(new[3])
        new[3] = new[3] - latent_heat * (evap * load)
        new[4] = new[4] / (1.0 + scavenge * load)
        for f in range(NF):
            fields[f, x] = new[f]
        by = kept * (1.0 - evap)
        plus = (spray_0[x] * kept + sprays) * (1.0 - evap)
        for k in range(slots):
            before = above[k, x] if x < 2 else mass[k, x - 2]
            masses[k, x] = jnp.where(held > k, before * by + plus, before)
        copy = pltpu.make_async_copy(masses.at[:, x], mass_out.at[:, x], sems.at[x])
        copy.start()
        pending.append(copy)
        if x % half == half - 1:
            done = slice(x + 1 - half, x + 1)
            pending += copies(
                [
                    (fields.at[0:3, done], wind_out.at[:, done]),
                    (fields.at[3, done], heat_out.at[done]),
                    (fields.at[4, done], soot_out.at[done]),
                ],
                sems.at[depth + 3 * (x // half) : depth + 3 * (x // half) + 3],
            )
    for copy in pending:
        copy.wait()

def last(got_x, got_y, above, own_low, own_high, mass, count, got_a, got_b, loads, spray_0, spray_1, nxt, nxt_nu, keep):
    block = count.shape
    operands = on_chip(got_x, got_y, above, own_low, own_high, mass, count, got_a, got_b, loads, spray_0, spray_1, nxt, nxt_nu, keep)
    return pl.pallas_call(
        last_kernel,
        out_shape=(
            jax.ShapeDtypeStruct((3,) + block, F32),
            jax.ShapeDtypeStruct(block, F32),
            jax.ShapeDtypeStruct(block, F32),
            jax.ShapeDtypeStruct(mass.shape, F32),
            pltpu.VMEM(nxt.shape, F32),
            pltpu.VMEM(nxt_nu.shape, F32),
            pltpu.VMEM(keep.shape, F32),
        ),
        in_specs=[VMEM] * 15,
        out_specs=(ANY,) * 4 + (VMEM,) * 3,
        input_output_aliases={12: 4, 13: 5, 14: 6},
        scratch_shapes=[
            pltpu.VMEM((2, NF, block[0] + 16, block[2]), F32),
            pltpu.VMEM(got_x.shape, F32),
            pltpu.VMEM(got_x.shape, F32),
            pltpu.VMEM((NF,) + block, F32),
            pltpu.VMEM(mass.shape, F32),
            pltpu.SemaphoreType.DMA((6 + block[0],)),
        ],
        compiler_params=LIMIT,
        cost_estimate=cost(LAST_COST),
        name="last_substep",
    )(*operands)[:4]


def local(wind, heat, soot, mass, count, label, onset):
    chain, width = lax.axis_size("tun"), lax.axis_size("sec")
    pairs_a = [(i, i ^ 1) for i in range(chain)]
    pairs_b = [(i, ((i + 1) ^ 1) - 1) for i in range(1, chain - 1)]
    msg_b, msg_a, tops, begins = pack_tun(onset, wind, heat, soot, mass, count, label)
    got_b = lax.ppermute(msg_b, "tun", pairs_b)
    got_a = lax.ppermute(msg_a, "tun", pairs_a)
    msg_x, msg_y, own_low, own_high = pack_sec(wind, heat, soot, mass, count, begins, got_a, got_b)
    got_x = lax.ppermute(msg_x, "sec", [(i, i ^ 1) for i in range(width)])
    got_y = lax.ppermute(msg_y, "sec", [(i, ((i + 1) ^ 1) - 1) for i in range(1, width - 1)])
    above = lax.ppermute(pack_mass(tops, begins), "tun", [(i, i + 1) for i in range(chain - 1)])
    count_out, nxt, nxt_nu, keep, loads, spray_0, spray_1 = first(
        wind, heat, soot, mass, count, begins, got_a, got_b, own_low
    )
    wind_out, heat_out, soot_out, mass_out = last(
        got_x, got_y, above, own_low, own_high, mass, count, got_a, got_b, loads, spray_0, spray_1, nxt, nxt_nu, keep
    )
    return wind_out, heat_out, soot_out, mass_out, count_out


def solution(mesh):
    return jax.shard_map(
        local,
        mesh=mesh,
        in_specs=(
            P(None, "tun", "sec", None),
            P("tun", "sec", None),
            P("tun", "sec", None),
            P(None, "tun", "sec", None),
            P("tun", "sec", None),
            P("tun", "sec", None),
            P(),
        ),
        out_specs=(
            P(None, "tun", "sec", None),
            P("tun", "sec", None),
            P("tun", "sec", None),
            P(None, "tun", "sec", None),
            P("tun", "sec", None),
        ),
        check_vma=False,
    )
```
